32 devices in a mesh: trial: 8 (over z, core), slab: 2 (over y), freq: 2 (over x).
Axes of the slice: x: 2, y: 2, z: 4, core: 2. Of those that a mesh axis runs over, the one named last changes fastest.
Arguments:
- orbitals: float32 [8, 8, 64, 128], P('trial', 'slab'), may hold values from -6 to 6
- energies: float32 [8], P('trial'), may hold values from 0 to 1
- potential: float32 [8, 64, 128], P('slab'), may hold values from 0 to 1
- trials: float32 [64, 8, 64, 128], P('trial', 'slab'), may hold values from -6 to 6
- cheb: float32 [2, 4], P('freq'), may hold values from 0.3 to 1
- shifts: float32 [2], P('freq'), may hold values from -0.5 to 0.5
- column_order: int32 [64], replicated, may hold values from 0 to 63, each once
Outputs:
- gram: float32 [64, 64], P(('trial', 'slab'))
The draws below stay inside these ranges and needn't reach their ends.
Inputs may be any that keep to these rules, and one draw needn't show every extreme that they name: `column_order`: each of 0 to 63 appears once.
All inputs are finite; a program needn't handle non-finite values.
Results may differ from the reference program's by a relative error of at most 0.00024.
Values sent between devices are 32-bit elements; how exact they have to be, the bound alone decides.
A program may use at most 64 MiB of HBM per device.

```python
import math
import jax
import jax.numpy as jnp
from jax import lax

NY = 64
NZ = 128
KSTEPS = 3
FREQS = 2
TRIALS = 64
NORB = 8
NX = 8


def plane_profile(key, rows):
    phase = jax.random.uniform(key, (rows, 1), jnp.float32, -math.pi, math.pi)
    plane = jnp.arange(NX).astype(jnp.float32)
    profile = 1.0 + 0.3 * jnp.sin(2.0 * math.pi * plane[None] / NX + phase)
    return profile[:, :, None, None]


def draw_orbitals(key, part):
    key_phase = jax.random.fold_in(key, 11)
    key_column = jax.random.fold_in(key, 12)
    key_rough = jax.random.fold_in(key, 13)
    profile = plane_profile(key_phase, NORB)
    column = jnp.clip(jax.random.normal(key_column, (NORB, 1, NY, NZ), jnp.float32), -2.5, 2.5)
    rough = 0.7 * jnp.clip(jax.random.normal(key_rough, (NORB, NX, NY, NZ), jnp.float32), -3.0, 3.0)
    return (profile * column + rough).astype(jnp.float32)


def draw_trials(key, part):
    key_phase = jax.random.fold_in(key, 21)
    key_column = jax.random.fold_in(key, 22)
    key_rough = jax.random.fold_in(key, 23)
    profile = plane_profile(key_phase, TRIALS)
    column = jnp.clip(jax.random.normal(key_column, (TRIALS, 1, NY, NZ), jnp.float32), -2.5, 2.5)
    rough = 0.7 * jnp.clip(jax.random.normal(key_rough, (TRIALS, NX, NY, NZ), jnp.float32), -3.0, 3.0)
    return (profile * column + rough).astype(jnp.float32)


def level_of(key, extent, split, smallest, high):
    factor_of = 1.0
    for position, shards_of in split:
        heights = jax.random.uniform(jax.random.fold_in(jax.random.fold_in(key, 6), position), (shards_of,), jnp.float32, smallest / len(split), high / len(split))
        factor_of = factor_of * jnp.repeat(jnp.exp(heights), extent[position] // shards_of).reshape((-1,) + (1,) * (len(extent) - 1 - position))
    return factor_of


def setup_inputs(seed: int = 0) -> dict:
    key_list = jax.random.split(jax.random.key(seed), 8)
    orbitals = draw_orbitals(jax.random.fold_in(key_list[7], 71), 0)
    energies = jnp.clip(1.0 * jax.random.uniform(key_list[1], (NORB,), jnp.float32) ** level_of(key_list[1], (NORB,), ((0, 8),), -0.2, 0.2), 0.0, 1.0)
    potential = jnp.clip(1.0 * jax.random.uniform(key_list[2], (NX, NY, NZ), jnp.float32) ** level_of(key_list[2], (NX, NY, NZ), ((0, 2),), -0.2, 0.2), 0.0, 1.0)
    trials = draw_trials(jax.random.fold_in(key_list[7], 71), 0)
    cheb = jnp.clip(0.3 + 0.7 * jax.random.uniform(key_list[4], (FREQS, KSTEPS + 1), jnp.float32) ** level_of(key_list[4], (FREQS, KSTEPS + 1), ((0, 2),), -0.2, 0.2), 0.3, 1.0)
    shifts = jnp.clip(jax.random.uniform(key_list[5], (FREQS,), jnp.float32, -0.5, 0.5) * level_of(key_list[5], (FREQS,), ((0, 2),), -0.4, 0.0), -0.5, 0.5)
    column_order = jax.random.permutation(key_list[6], TRIALS).astype(jnp.int32)
    return {"orbitals": orbitals, "energies": energies, "potential": potential, "trials": trials, "cheb": cheb, "shifts": shifts, "column_order": column_order}


def apply_op(field, coef):
    padded = jnp.pad(field, ((0, 0), (1, 1), (1, 1), (1, 1)))
    beside = padded[:, 2:, 1:-1, 1:-1] + padded[:, :-2, 1:-1, 1:-1]
    beside = beside + padded[:, 1:-1, 2:, 1:-1] + padded[:, 1:-1, :-2, 1:-1]
    beside = beside + padded[:, 1:-1, 1:-1, 2:] + padded[:, 1:-1, 1:-1, :-2]
    return (coef[None] * field - 0.5 * beside) / 4.5

def reference(orbitals, energies, potential, trials, cheb, shifts, column_order):
    norb = orbitals.shape[0]

    def one_orbital(carry, item):
        orbital, energy = item
        start = orbital[None] * trials
        parts = []
        for freq in range(FREQS):
            coef = potential - energy - shifts[freq]
            before = start
            now = apply_op(start, coef)
            response = cheb[freq, 0] * start + cheb[freq, 1] * now
            for order in range(2, KSTEPS + 1):
                after = 2.0 * apply_op(now, coef) - before
                response = response + cheb[freq, order] * after
                before, now = (now, after)
            parts.append(orbital[None] * response)
        return (carry + jnp.stack(parts), None)
    empty = jnp.zeros((FREQS, TRIALS, NX, NY, NZ), jnp.float32)
    density, _ = lax.scan(one_orbital, empty, (orbitals, energies))
    total = lax.optimization_barrier(jnp.sum(density, axis=0))
    left = trials.reshape(TRIALS, -1)[column_order]
    right = total.reshape(TRIALS, -1)[column_order]
    gram = jnp.dot(left, right.T, precision=lax.Precision.HIGHEST, preferred_element_type=jnp.float32)
    return gram / jnp.sqrt(jnp.float32(NX * NY * NZ * norb))
```

```python
import functools

import jax
import jax.numpy as jnp
from jax import lax
from jax.experimental import pallas as pl
from jax.experimental.pallas import tpu as pltpu
from jax.sharding import PartitionSpec as P

REACH = 3
UNDER = 2
MESH = pl.DeviceIdType.MESH
HIGH = lax.Precision.HIGHEST

OFFSETS = [
    (dx, dy, dz)
    for dz in range(-REACH, REACH + 1)
    for dx in range(-REACH, REACH + 1)
    for dy in range(REACH + 1)
    if abs(dx) + abs(dy) + abs(dz) <= REACH and (dy, dx, dz) >= (0, 0, 0)
]
PATHS = {(1, 1, 1): 6.0, (0, 1, 2): 3.0, (0, 0, 3): 1.0}
PIECES = 2


def rolled(value, shift):
    shift = shift % value.shape[1]
    return value if shift == 0 else pltpu.roll(value, shift, 1)


def when(condition, action):
    pl.when(condition)(action)


def kernel(
    sizes, orb, ene, pot, tri, che, shi, order, out,
    orbs, wide, other, pots, pars, freqs, weights, coefs, dens, rows_out, rows_in,
    ene_m, che_m, shi_m, picks,
    orb_s, orb_r, par_s, par_r, pot_s, pot_r, frq_s, frq_r,
    tri_s, tri_r, fwd_s, fwd_r, row_s, row_r, loc, gate,
):
    nt, ns, nf = sizes
    per, planes, ny, nz = tri.shape
    norb = orbs.shape[0]
    half = ny // nf
    total = nt * per
    chips = nt // 2
    mine = half // chips
    tall = mine + REACH
    some = per // PIECES
    deep = planes + UNDER + REACH
    t, s, f = lax.axis_index("trial"), lax.axis_index("slab"), lax.axis_index("freq")
    z, c = t // 2, lax.rem(t, 2)
    mate = t + 1 - 2 * c
    first, last = s == 0, s == ns - 1
    up, down = s < ns - 1, s > 0
    inner = slice(UNDER, UNDER + planes)
    over, under = slice(UNDER + planes, deep), slice(0, UNDER)
    near = ns <= 2 and nf <= 2
    y_mine = f * half + z * mine

    def beyond(zz):
        return (f == nf - 1) & (zz == chips - 1)

    def sized(zz, action):
        when(beyond(zz), lambda: action(mine))
        when(jnp.logical_not(beyond(zz)), lambda: action(tall))

    wrows = min(mine + 16, ny)
    y_pot = jnp.clip(y_mine - 8, 0, ny - wrows)
    win = pl.ds(y_pot, wrows)
    win_to = pl.ds(y_pot + 8, wrows)

    def own_orb(rows):
        return pltpu.make_async_copy(orb.at[0, :, pl.ds(y_mine, rows), :], orbs.at[t, inner, :rows, :], loc.at[0])

    def own_tri(rows):
        return pltpu.make_async_copy(tri.at[:, :, pl.ds(y_mine, rows), :], wide.at[z, :, inner, :rows, :], loc.at[1])

    locals_ = [
        pltpu.make_async_copy(ene, ene_m, loc.at[2]),
        pltpu.make_async_copy(che, che_m, loc.at[3]),
        pltpu.make_async_copy(shi, shi_m, loc.at[4]),
        pltpu.make_async_copy(pot.at[:, win, :], pots.at[2 : planes + 2, win_to, :], loc.at[5]),
        pltpu.make_async_copy(order, picks, loc.at[6]),
    ]
    for copy in locals_[:3]:
        copy.start()
    sized(z, lambda rows: own_orb(rows).start())
    for copy in locals_[3:]:
        copy.start()
    sized(z, lambda rows: own_tri(rows).start())

    def device(k):
        dt, ds, df = k // (ns * nf), (k // nf) % ns, k % nf
        return lax.rem(t + dt, nt), lax.rem(s + ds, ns), lax.rem(f + df, nf)

    count = nt * ns * nf
    barrier = pltpu.get_barrier_semaphore()
    below, above = jnp.maximum(s - 1, 0), jnp.minimum(s + 1, ns - 1)
    if chips == 4:
        hops = [2, 3 - 2 * lax.rem(z, 2), 1 + 2 * lax.rem(z, 2)]
        backs = [2, 3 - 2 * lax.rem(z, 2), 1 + 2 * lax.rem(z, 2)]
    else:
        hops = list(range(1, chips))
        backs = [chips - k for k in hops]
    peers = [lax.rem(z + k, chips) for k in hops]
    froms = [lax.rem(z + k, chips) for k in backs]

    def greet(**where):
        pl.semaphore_signal(barrier, inc=1, device_id=where, device_id_type=MESH)

    pots[:, 0:8, :] = jnp.zeros((planes + 4, 8, nz), jnp.float32)
    pots[:, ny + 8 :, :] = jnp.zeros((planes + 4, 8, nz), jnp.float32)

    @pl.when(last)
    def _():
        orbs[:, over] = jnp.zeros((norb, REACH) + orbs.shape[2:], jnp.float32)
        wide[:, :, over] = jnp.zeros((chips, per, REACH) + wide.shape[3:], jnp.float32)
        pots[planes + 2 :] = jnp.zeros((2,) + pots.shape[1:], jnp.float32)

    @pl.when(first)
    def _():
        orbs[:, under] = jnp.zeros((norb, UNDER) + orbs.shape[2:], jnp.float32)
        wide[:, :, under] = jnp.zeros((chips, per, UNDER) + wide.shape[3:], jnp.float32)
        pots[:2] = jnp.zeros((2,) + pots.shape[1:], jnp.float32)

    @pl.when(beyond(z))
    def _():
        orbs[:, :, mine:tall, :] = jnp.zeros((norb, deep, REACH, nz), jnp.float32)
        wide[:, :, :, mine:tall, :] = jnp.zeros((chips, per, deep, REACH, nz), jnp.float32)

    if near:
        for p in peers:
            greet(trial=2 * p + c)
        greet(trial=mate)
        for j in range(1, ns):
            greet(slab=lax.rem(s + j, ns))
        for j in range(1, nf):
            greet(freq=lax.rem(f + j, nf))
        greeted = chips + ns + nf - 2
    else:

        @pl.loop(1, count)
        def _(k):
            pt, ps, pf = device(k)
            greet(trial=pt, slab=ps, freq=pf)

        greeted = count - 1

    for copy in locals_[:3]:
        copy.wait()
    pars[t] = jnp.full((8, nz), ene_m[0], jnp.float32)
    row = lax.broadcasted_iota(jnp.int32, (8, nz), 0)
    tile = jnp.full((8, nz), shi_m[0], jnp.float32)
    for n in range(4):
        tile = jnp.where(row == n, che_m[0, n], tile)
    freqs[f] = tile
    sized(z, lambda rows: own_orb(rows).wait())

    pl.semaphore_wait(barrier, greeted)

    def remote(src, dst, send, recv, **where):
        return pltpu.make_async_remote_copy(
            src_ref=src, dst_ref=dst, send_sem=send, recv_sem=recv, device_id=where, device_id_type=MESH
        )

    def rows_at(p, rows):
        return pl.ds(f * half + p * mine, rows)

    def orb_out(p, rows):
        source = orb.at[0, :, rows_at(p, rows), :]
        return remote(source, orbs.at[t, inner, :rows, :], orb_s.at[p, 0], orb_r.at[t, 0], trial=2 * p + c)

    def orb_in(p, rows):
        block = orbs.at[2 * p + c, inner, :rows, :]
        return remote(block, block, orb_s.at[p, 0], orb_r.at[2 * p + c, 0], trial=mate)

    def orb_mate(u, rows):
        block = orbs.at[u, inner, :rows, :]
        return remote(block, block, orb_s.at[u // 2, 1], orb_r.at[u, 0], trial=mate)

    def short(rows):
        return min(rows, mine + 2)

    def orb_halo(p, way, rows):
        u = 2 * p + c
        n = short(rows)
        if way == 0:
            source, there = orbs.at[u, planes : planes + UNDER, :n, :], orbs.at[u, under, :n, :]
            return remote(source, there, orb_s.at[p, 2], orb_r.at[u, 1], slab=above)
        source, there = orbs.at[u, UNDER : UNDER + REACH, :n, :], orbs.at[u, over, :n, :]
        return remote(source, there, orb_s.at[p, 3], orb_r.at[u, 2], slab=below)

    def halo_mate(u, way, rows):
        block = orbs.at[u, under if way == 0 else over, : short(rows), :]
        return remote(block, block, orb_s.at[u // 2, 4 + way], orb_r.at[u, 1 + way], trial=mate)

    def par_out(p):
        return remote(pars.at[t], pars.at[t], par_s.at[p], par_r.at[t], trial=2 * p + c)

    def par_mate(p, u):
        return remote(pars.at[u], pars.at[u], par_s.at[chips + p], par_r.at[u], trial=mate)

    def pot_halo(way):
        if way == 0:
            source, there = pot.at[planes - 2 :, win, :], pots.at[:2, win_to, :]
            return remote(source, there, pot_s.at[0], pot_r.at[0], slab=above)
        source, there = pot.at[:2, win, :], pots.at[planes + 2 :, win_to, :]
        return remote(source, there, pot_s.at[1], pot_r.at[1], slab=below)

    def freq_copy(j):
        return remote(freqs.at[f], freqs.at[f], frq_s.at[j], frq_r.at[j], freq=lax.rem(f + j, nf))

    def part(q):
        return slice(q * some, (q + 1) * some)

    def tri_out(p, q, rows):
        source = tri.at[part(q), :, rows_at(p, rows), :]
        there = wide.at[z, part(q), inner, :rows, :]
        return remote(source, there, tri_s.at[p, q], tri_r.at[z, q], trial=2 * p + c)

    def tri_in(p, q, rows):
        block = wide.at[p, part(q), inner, :rows, :]
        return remote(block, block, tri_s.at[p, q], tri_r.at[p, q], trial=mate)

    def tri_mate(p, q):
        source = wide.at[p, part(q), inner, :mine, :]
        return remote(source, other.at[p, part(q)], fwd_s.at[p, q, 0], fwd_r.at[p, q, 0], trial=mate)

    def tri_halo(p, q, way, rows):
        n = short(rows)
        if way == 0:
            source, there = wide.at[p, part(q), planes : planes + UNDER, :n, :], wide.at[p, part(q), under, :n, :]
            return remote(source, there, fwd_s.at[p, q, 1], fwd_r.at[p, q, 1], slab=above)
        source, there = wide.at[p, part(q), UNDER : UNDER + REACH, :n, :], wide.at[p, part(q), over, :n, :]
        return remote(source, there, fwd_s.at[p, q, 2], fwd_r.at[p, q, 2], slab=below)

    def orb_spread(p):
        u = 2 * p + c
        sized(z, lambda rows: when(down, lambda: orb_halo(p, 1, rows).start()))
        sized(z, lambda rows: when(up, lambda: orb_halo(p, 0, rows).start()))
        sized(z, lambda rows: orb_mate(u, rows).start())
        par_mate(p, u).start()

    def tri_spread(p, q):
        sized(z, lambda rows: when(down, lambda: tri_halo(p, q, 1, rows).start()))
        sized(z, lambda rows: when(up, lambda: tri_halo(p, q, 0, rows).start()))
        tri_mate(p, q).start()

    for p in peers:
        sized(p, lambda rows: orb_out(p, rows).start())
        par_out(p).start()
    orb_spread(z)
    for j in range(1, nf):
        freq_copy(j).start()
    when(up, lambda: pot_halo(0).start())
    when(down, lambda: pot_halo(1).start())
    units = [(n, q) for n in range(chips - 1) for q in range(PIECES)]
    for n, q in units:
        sized(peers[n], lambda rows: tri_out(peers[n], q, rows).start())

    for p in froms:
        sized(z, lambda rows: orb_in(p, rows).wait_recv())
        par_mate(p, 2 * p + c).wait_recv()
        orb_spread(p)
    sized(z, lambda rows: own_tri(rows).wait())
    for q in range(PIECES):
        tri_spread(z, q)
    for p in [z] + froms:

        def pass_on(rows):
            def side(way):
                halo_mate(2 * p + c, way, rows).wait_recv()
                halo_mate(2 * p + c, way, rows).start()

            when(up, lambda: side(1))
            when(down, lambda: side(0))

        sized(z, pass_on)

    for copy in locals_[3:]:
        copy.wait()
    for j in range(1, nf):
        freq_copy(j).wait_recv()
    for j in range(chips):
        u = 2 * j + 1 - c

        def waits(rows):
            orb_mate(u, rows).wait_recv()
            when(up, lambda: halo_mate(u, 1, rows).wait_recv())
            when(down, lambda: halo_mate(u, 0, rows).wait_recv())

        sized(z, waits)
        par_mate(j, u).wait_recv()
    if near:
        for j in range(1, nf):
            pl.semaphore_signal(gate, inc=1, device_id={"freq": lax.rem(f + j, nf)}, device_id_type=MESH)
    when(up, lambda: pot_halo(1).wait_recv())
    when(down, lambda: pot_halo(0).wait_recv())

    inverse = 1.0 / 4.5
    hop = -0.5 / 4.5

    for i in range(norb):
        energy = pars[i]
        terms = [0.0, 0.0, 0.0, 0.0]
        for w in range(nf):
            mu = (energy + freqs[w, 4:5, :]) * inverse
            c0, c1, c2, c3 = (freqs[w, n : 1 + n, :] for n in range(4))
            b0, b1, b2, b3 = c0 - c2, c1 - 3.0 * c3, 2.0 * c2, 4.0 * c3
            terms[0] += b0 - mu * (b1 - mu * (b2 - mu * b3))
            terms[1] += b1 - mu * (2.0 * b2 - 3.0 * mu * b3)
            terms[2] += b2 - 3.0 * mu * b3
            terms[3] += b3
        for n in range(4):
            weights[n, i] = jnp.broadcast_to(terms[n], (8, nz))

    lane = lax.broadcasted_iota(jnp.int32, (mine, nz), 1)
    rows_ = lax.broadcasted_iota(jnp.int32, (mine, nz), 0) + y_mine

    def links(position, size):
        return (position >= 1).astype(jnp.float32) + (position + 1 < size).astype(jnp.float32)

    def coef_plane(x, carry):
        column = jnp.zeros((mine, nz), jnp.int32) + (s * planes + x)
        for dz in range(-REACH, REACH + 1):
            group = [(n, off) for n, off in enumerate(OFFSETS) if off[2] == dz]
            if not group:
                continue
            depth = lane - dz
            inside = ((depth >= 0) & (depth < nz)).astype(jnp.float32)
            least = min(sum(map(abs, off)) for _, off in group)
            scaled = {}
            for i in range(norb):
                centre = rolled(orbs[i, UNDER + x, :mine, :], dz) * inside
                for n in range(least, 4):
                    scaled[n, i] = weights[n, i, :mine, :] * centre

            def local(a, b, e):
                return rolled(pots[2 + x + a, pl.ds(8 + y_mine + b, mine), :], dz - e) * inverse

            for index, (dx, dy, _) in group:
                steps = abs(dx) + abs(dy) + abs(dz)
                sums = {n: 0.0 for n in range(steps, 4)}
                for i in range(norb):
                    there = orbs[i, UNDER + x + dx, dy : dy + mine, :]
                    for n in sums:
                        sums[n] = sums[n] + scaled[n, i] * there
                if steps == 3:
                    kind = tuple(sorted(map(abs, (dx, dy, dz))))
                    coef = (PATHS[kind] * hop**3) * sums[3]
                elif steps == 2:
                    here, end = local(0, 0, 0), local(dx, dy, dz)
                    corners = [p for p in ((dx, 0, 0), (0, dy, 0), (0, 0, dz)) if p != (0, 0, 0)]
                    if len(corners) == 1:
                        middle = local(int(dx / 2), int(dy / 2), int(dz / 2))
                        coef = hop**2 * (sums[2] + (here + middle + end) * sums[3])
                    else:
                        middle = local(*corners[0]) + local(*corners[1])
                        coef = hop**2 * (2.0 * sums[2] + (2.0 * (here + end) + middle) * sums[3])
                elif steps == 1:
                    here, end = local(0, 0, 0), local(dx, dy, dz)
                    place = (column, rows_, depth)
                    size = (planes * ns, ny, nz)
                    move = (dx, dy, dz)
                    side, along = 0.0, 0.0
                    for axis in range(3):
                        if move[axis]:
                            along = links(place[axis], size[axis]) + links(place[axis] + move[axis], size[axis])
                        else:
                            side = side + links(place[axis], size[axis])
                    walks = along + 3.0 * side - 1.0
                    cubic = here * here + here * end + end * end + hop**2 * walks
                    coef = hop * (sums[1] + (here + end) * sums[2] + cubic * sums[3])
                else:
                    here = local(0, 0, 0)
                    degree = links(column, planes * ns) + links(rows_, ny) + links(lane, nz)
                    beside = local(1, 0, 0) + local(-1, 0, 0) + local(0, 1, 0) + local(0, -1, 0)
                    beside = beside + jnp.where(lane + 1 < nz, local(0, 0, 1), 0.0)
                    beside = beside + jnp.where(lane >= 1, local(0, 0, -1), 0.0)
                    square = here * here + hop**2 * degree
                    cube = here * (here * here + 2.0 * hop**2 * degree) + hop**2 * beside
                    coef = 0.5 * (sums[0] + here * sums[1] + square * sums[2] + cube * sums[3])
                coefs[x, index] = coef
        return carry

    lax.fori_loop(0, planes, coef_plane, 0)

    def density(p, q):
        def halos(rows):
            when(up, lambda: tri_halo(p, q, 1, rows).wait_recv())
            when(down, lambda: tri_halo(p, q, 0, rows).wait_recv())

        sized(z, halos)

        def plane_step(x, carry):
            sums_ = [0.0] * some
            for dz in range(-REACH, REACH + 1):
                group = [(n, off) for n, off in enumerate(OFFSETS) if off[2] == dz]
                if not group:
                    continue
                sums = [0.0] * some
                for index, (dx, dy, _) in group:
                    coef = coefs[x, index]
                    for k in range(some):
                        sums[k] = sums[k] + coef * wide[p, q * some + k, UNDER + x + dx, dy : dy + mine, :]
                for k in range(some):
                    sums_[k] = sums_[k] + rolled(sums[k], -dz)
            for k in range(some):
                dens[p, q * some + k, x] = sums_[k]
            return carry

        lax.fori_loop(0, planes, plane_step, 0)

    def take(n, q):
        sized(z, lambda rows: tri_in(froms[n], q, rows).wait_recv())
        tri_spread(froms[n], q)

    work = [(z, q) for q in range(PIECES)] + [(froms[n], q) for n, q in units]
    for step in range(len(units)):
        take(*units[step])
        density(*work[step])
    for step in range(len(units), len(work)):
        density(*work[step])
    for j in range(chips):
        for q in range(PIECES):
            tri_mate(j, q).wait_recv()

    contract = (((1,), (1,)), ((), ()))
    part_ = chips * per

    def gram_plane(x, acc):
        for r in range(mine):
            ours = wide[:, :, UNDER + x, r, :].reshape(part_, nz)
            theirs = other[:, :, x, r, :].reshape(part_, nz)
            right = dens[:, :, x, r, :].reshape(part_, nz)
            acc = acc + lax.dot_general(
                jnp.concatenate([ours, theirs], axis=0), right, contract,
                precision=HIGH, preferred_element_type=jnp.float32,
            )
        return acc

    gram = lax.fori_loop(0, planes, gram_plane, jnp.zeros((total, part_), jnp.float32))
    index = lax.broadcasted_iota(jnp.int32, (total, total), 0)
    theirs = index // part_
    place = lax.rem(index, part_)
    trial = (2 * (place // per) + c + theirs * (1 - 2 * c)) * per + lax.rem(place, per)
    pick = (picks[...] == trial).astype(jnp.float32)
    factor = 1.0 / jnp.sqrt(jnp.float32(planes * ns * ny * nz * norb))
    moved = lax.dot_general(
        pick, gram * factor, (((0,), (0,)), ((), ())), precision=HIGH, preferred_element_type=jnp.float32
    )
    final = jnp.dot(moved, pick[:part_], precision=HIGH, preferred_element_type=jnp.float32)
    final = final + final.T
    owned = total // (nt * ns)
    for r in range(nt * ns):
        rows_out[r] = final[r * owned : (r + 1) * owned]
    if near:
        for j in range(1, nf):
            pl.semaphore_wait(gate, 1)

    def me():
        return (t * ns + s) * nf + f

    def row_copy(k):
        pt, ps, pf = device(k)
        return remote(
            rows_out.at[pt * ns + ps], rows_in.at[me()], row_s.at[k], row_r.at[k], trial=pt, slab=ps, freq=pf
        )

    def each(action):
        if count <= 64:
            for k in range(1, count):
                action(k)
        else:
            pl.loop(1, count)(action)

    each(lambda k: row_copy(k).start())
    rows_in[me()] = rows_out[t * ns + s]
    for j in range(1, nf):
        freq_copy(j).wait_send()
    when(up, lambda: pot_halo(0).wait_send())
    when(down, lambda: pot_halo(1).wait_send())
    for n, p in enumerate(peers):
        par_out(p).wait_send()

        def out_waits(rows):
            orb_out(p, rows).wait_send()
            for q in range(PIECES):
                tri_out(p, q, rows).wait_send()

        sized(p, out_waits)

    def sends(rows):
        for p in range(chips):
            u = 2 * p + c
            orb_mate(u, rows).wait_send()

            @pl.when(up)
            def _():
                orb_halo(p, 0, rows).wait_send()
                halo_mate(u, 1, rows).wait_send()
                for q in range(PIECES):
                    tri_halo(p, q, 0, rows).wait_send()

            @pl.when(down)
            def _():
                orb_halo(p, 1, rows).wait_send()
                halo_mate(u, 0, rows).wait_send()
                for q in range(PIECES):
                    tri_halo(p, q, 1, rows).wait_send()

    sized(z, sends)
    for p in range(chips):
        par_mate(p, 2 * p + c).wait_send()
        for q in range(PIECES):
            tri_mate(p, q).wait_send()
    each(lambda k: row_copy(k).wait())
    out[...] = jnp.sum(rows_in[...], axis=0)


def local(sizes, orbitals, energies, potential, trials, cheb, shifts, column_order):
    nt, ns, nf = sizes
    per, planes, ny, nz = trials.shape
    norb = orbitals.shape[0] * nt
    chips = nt // 2
    mine = ny // nf // chips
    tall = -(-(mine + REACH) // 8) * 8
    deep = planes + UNDER + REACH
    total = nt * per
    owned = total // (nt * ns)
    count = nt * ns * nf
    f32 = jnp.float32
    dma = pltpu.SemaphoreType.DMA
    anywhere = pl.BlockSpec(memory_space=pltpu.HBM)
    return pl.pallas_call(
        functools.partial(kernel, sizes),
        out_shape=jax.ShapeDtypeStruct((owned, total), f32),
        in_specs=[anywhere] * 7,
        out_specs=pl.BlockSpec(memory_space=pltpu.VMEM),
        scratch_shapes=[
            pltpu.VMEM((norb, deep, tall, nz), f32),
            pltpu.VMEM((chips, per, deep, tall, nz), f32),
            pltpu.VMEM((chips, per, planes, mine, nz), f32),
            pltpu.VMEM((planes + 4, ny + 16, nz), f32),
            pltpu.VMEM((norb, 8, nz), f32),
            pltpu.VMEM((nf, 8, nz), f32),
            pltpu.VMEM((4, norb, 8, nz), f32),
            pltpu.VMEM((planes, len(OFFSETS), mine, nz), f32),
            pltpu.VMEM((chips, per, planes, mine, nz), f32),
            pltpu.VMEM((nt * ns, owned, total), f32),
            pltpu.VMEM((count, owned, total), f32),
            pltpu.SMEM((1,), f32),
            pltpu.SMEM((1, 4), f32),
            pltpu.SMEM((1,), f32),
            pltpu.VMEM((1, total), jnp.int32),
            dma((chips, 6)), dma((nt, 3)), dma((2 * chips,)), dma((nt,)),
            dma((2,)), dma((2,)), dma((nf,)), dma((nf,)),
            dma((chips, PIECES)), dma((chips, PIECES)), dma((chips, PIECES, 3)), dma((chips, PIECES, 3)),
            dma((count,)), dma((count,)),
            dma((7,)),
            pltpu.SemaphoreType.REGULAR,
        ],
        compiler_params=pltpu.CompilerParams(
            collective_id=0, has_side_effects=True, vmem_limit_bytes=67043328 - 65536
        ),
    )(orbitals, energies, potential, trials, cheb, shifts, column_order[None])


def solution(mesh):
    sizes = tuple(mesh.shape[name] for name in ("trial", "slab", "freq"))
    in_specs = (
        P("trial", "slab", None, None),
        P("trial"),
        P("slab", None, None),
        P("trial", "slab", None, None),
        P("freq", None),
        P("freq"),
        P(),
    )
    out_specs = P(("trial", "slab"), None)
    return jax.shard_map(
        functools.partial(local, sizes), mesh=mesh, in_specs=in_specs, out_specs=out_specs, check_vma=False
    )
```

```python
import functools

import jax
import jax.numpy as jnp
from jax import lax
from jax.experimental import pallas as pl
from jax.experimental.pallas import tpu as pltpu
from jax.sharding import PartitionSpec as P

REACH = 3
UNDER = 2
MESH = pl.DeviceIdType.MESH
HIGH = lax.Precision.HIGHEST

OFFSETS = [
    (dx, dy, dz)
    for dz in range(-REACH, REACH + 1)
    for dx in range(-REACH, REACH + 1)
    for dy in range(REACH + 1)
    if abs(dx) + abs(dy) + abs(dz) <= REACH and (dy, dx, dz) >= (0, 0, 0)
]
PATHS = {(1, 1, 1): 6.0, (0, 1, 2): 3.0, (0, 0, 3): 1.0}
PIECES = 2


def rolled(value, shift):
    shift = shift % value.shape[1]
    return value if shift == 0 else pltpu.roll(value, shift, 1)


def when(condition, action):
    pl.when(condition)(action)


def kernel(
    sizes, orb, ene, pot, tri, che, shi, order, out,
    orbs, wide, other, pots, pars, freqs, weights, coefs, dens, rows_out, rows_in,
    ene_m, che_m, shi_m, picks,
    orb_s, orb_r, par_s, par_r, pot_s, pot_r, frq_s, frq_r,
    tri_s, tri_r, fwd_s, fwd_r, row_s, row_r, loc, gate,
):
    nt, ns, nf = sizes
    per, planes, ny, nz = tri.shape
    norb = orbs.shape[0]
    half = ny // nf
    total = nt * per
    chips = nt // 2
    mine = half // chips
    tall = mine + REACH
    hp = planes // PIECES
    fore = min(REACH, hp)
    deep = planes + UNDER + REACH
    t, s, f = lax.axis_index("trial"), lax.axis_index("slab"), lax.axis_index("freq")
    z, c = t // 2, lax.rem(t, 2)
    mate = t + 1 - 2 * c
    first, last = s == 0, s == ns - 1
    up, down = s < ns - 1, s > 0
    inner = slice(UNDER, UNDER + planes)
    over, under = slice(UNDER + planes, deep), slice(0, UNDER)
    near = ns <= 2 and nf <= 2
    y_mine = f * half + z * mine

    def beyond(zz):
        return (f == nf - 1) & (zz == chips - 1)

    def sized(zz, action):
        when(beyond(zz), lambda: action(mine))
        when(jnp.logical_not(beyond(zz)), lambda: action(tall))

    wrows = min(mine + 16, ny)
    y_pot = jnp.clip(y_mine - 8, 0, ny - wrows)
    win = pl.ds(y_pot, wrows)
    win_to = pl.ds(y_pot + 8, wrows)

    def own_orb(rows):
        return pltpu.make_async_copy(orb.at[0, :, pl.ds(y_mine, rows), :], orbs.at[t, inner, :rows, :], loc.at[0])

    def own_tri(rows):
        return pltpu.make_async_copy(tri.at[:, :, pl.ds(y_mine, rows), :], wide.at[z, :, inner, :rows, :], loc.at[1])

    locals_ = [
        pltpu.make_async_copy(ene, ene_m, loc.at[2]),
        pltpu.make_async_copy(che, che_m, loc.at[3]),
        pltpu.make_async_copy(shi, shi_m, loc.at[4]),
        pltpu.make_async_copy(pot.at[:, win, :], pots.at[2 : planes + 2, win_to, :], loc.at[5]),
        pltpu.make_async_copy(order, picks, loc.at[6]),
    ]
    def device(k):
        dt, ds, df = k // (ns * nf), (k // nf) % ns, k % nf
        return lax.rem(t + dt, nt), lax.rem(s + ds, ns), lax.rem(f + df, nf)

    count = nt * ns * nf
    barrier = pltpu.get_barrier_semaphore()
    below, above = jnp.maximum(s - 1, 0), jnp.minimum(s + 1, ns - 1)
    if chips == 4:
        hops = [1 + 2 * lax.rem(z, 2), 2, 3 - 2 * lax.rem(z, 2)]
        backs = hops
    else:
        hops = list(range(1, chips))
        backs = [chips - k for k in hops]
    peers = [lax.rem(z + k, chips) for k in hops]
    froms = [lax.rem(z + k, chips) for k in backs]

    def greet(**where):
        pl.semaphore_signal(barrier, inc=1, device_id=where, device_id_type=MESH)

    if near:
        for p in peers:
            greet(trial=2 * p + c)
        greet(trial=mate)
        for j in range(1, ns):
            greet(slab=lax.rem(s + j, ns))
        for j in range(1, nf):
            greet(freq=lax.rem(f + j, nf))
        greeted = chips + ns + nf - 2
    else:

        @pl.loop(1, count)
        def _(k):
            pt, ps, pf = device(k)
            greet(trial=pt, slab=ps, freq=pf)

        greeted = count - 1

    for copy in locals_[:3]:
        copy.start()
    sized(z, lambda rows: own_orb(rows).start())
    for copy in locals_[3:]:
        copy.start()
    sized(z, lambda rows: own_tri(rows).start())

    pots[:, 0:8, :] = jnp.zeros((planes + 4, 8, nz), jnp.float32)
    pots[:, ny + 8 :, :] = jnp.zeros((planes + 4, 8, nz), jnp.float32)

    @pl.when(last)
    def _():
        orbs[:, over] = jnp.zeros((norb, REACH) + orbs.shape[2:], jnp.float32)
        wide[:, :, over] = jnp.zeros((chips, per, REACH) + wide.shape[3:], jnp.float32)
        pots[planes + 2 :] = jnp.zeros((2,) + pots.shape[1:], jnp.float32)

    @pl.when(first)
    def _():
        orbs[:, under] = jnp.zeros((norb, UNDER) + orbs.shape[2:], jnp.float32)
        wide[:, :, under] = jnp.zeros((chips, per, UNDER) + wide.shape[3:], jnp.float32)
        pots[:2] = jnp.zeros((2,) + pots.shape[1:], jnp.float32)

    @pl.when(beyond(z))
    def _():
        orbs[:, :, mine:tall, :] = jnp.zeros((norb, deep, REACH, nz), jnp.float32)
        wide[:, :, :, mine:tall, :] = jnp.zeros((chips, per, deep, REACH, nz), jnp.float32)

    for copy in locals_[:3]:
        copy.wait()
    pars[t] = jnp.full((8, nz), ene_m[0], jnp.float32)
    row = lax.broadcasted_iota(jnp.int32, (8, nz), 0)
    tile = jnp.full((8, nz), shi_m[0], jnp.float32)
    for n in range(4):
        tile = jnp.where(row == n, che_m[0, n], tile)
    freqs[f] = tile
    sized(z, lambda rows: own_orb(rows).wait())

    pl.semaphore_wait(barrier, greeted)

    def remote(src, dst, send, recv, **where):
        return pltpu.make_async_remote_copy(
            src_ref=src, dst_ref=dst, send_sem=send, recv_sem=recv, device_id=where, device_id_type=MESH
        )

    def rows_at(p, rows):
        return pl.ds(f * half + p * mine, rows)

    def orb_out(p, rows):
        source = orb.at[0, :, rows_at(p, rows), :]
        return remote(source, orbs.at[t, inner, :rows, :], orb_s.at[p, 0], orb_r.at[t, 0], trial=2 * p + c)

    def orb_in(p, rows):
        block = orbs.at[2 * p + c, inner, :rows, :]
        return remote(block, block, orb_s.at[p, 0], orb_r.at[2 * p + c, 0], trial=mate)

    def orb_mate(u, rows):
        block = orbs.at[u, inner, :rows, :]
        return remote(block, block, orb_s.at[u // 2, 1], orb_r.at[u, 0], trial=mate)

    def short(rows):
        return min(rows, mine + 2)

    def orb_halo(p, way, rows):
        u = 2 * p + c
        n = short(rows)
        if way == 0:
            source, there = orbs.at[u, planes : planes + UNDER, :n, :], orbs.at[u, under, :n, :]
            return remote(source, there, orb_s.at[p, 2], orb_r.at[u, 1], slab=above)
        source, there = orbs.at[u, UNDER : UNDER + REACH, :n, :], orbs.at[u, over, :n, :]
        return remote(source, there, orb_s.at[p, 3], orb_r.at[u, 2], slab=below)

    def halo_mate(u, way, rows):
        block = orbs.at[u, under if way == 0 else over, : short(rows), :]
        return remote(block, block, orb_s.at[u // 2, 4 + way], orb_r.at[u, 1 + way], trial=mate)

    def par_out(p):
        return remote(pars.at[t], pars.at[t], par_s.at[p], par_r.at[t], trial=2 * p + c)

    def par_mate(p, u):
        return remote(pars.at[u], pars.at[u], par_s.at[chips + p], par_r.at[u], trial=mate)

    def pot_halo(way):
        if way == 0:
            source, there = pot.at[planes - 2 :, win, :], pots.at[:2, win_to, :]
            return remote(source, there, pot_s.at[0], pot_r.at[0], slab=above)
        source, there = pot.at[:2, win, :], pots.at[planes + 2 :, win_to, :]
        return remote(source, there, pot_s.at[1], pot_r.at[1], slab=below)

    def freq_copy(j):
        return remote(freqs.at[f], freqs.at[f], frq_s.at[j], frq_r.at[j], freq=lax.rem(f + j, nf))

    flip = first & (ns > 1)

    def pair(h):
        return jnp.where(flip, planes - hp * (h + 1), hp * h)

    def held(h):
        return pl.ds(UNDER + pair(h), hp)

    def tri_out(p, h, rows):
        source = tri.at[:, pl.ds(pair(h), hp), rows_at(p, rows), :]
        there = wide.at[z, :, held(h), :rows, :]
        return remote(source, there, tri_s.at[p, h], tri_r.at[z, h], trial=2 * p + c)

    def tri_in(p, h, rows):
        block = wide.at[p, :, held(h), :rows, :]
        return remote(block, block, tri_s.at[p, h], tri_r.at[p, h], trial=mate)

    def tri_mate(p, h):
        source = wide.at[p, :, held(h), :mine, :]
        there = other.at[p, :, pl.ds(pair(h), hp)]
        return remote(source, there, fwd_s.at[p, h, 0], fwd_r.at[p, 0, pair(h) // hp], trial=mate)

    def tri_halo(p, way, rows):
        n = short(rows) if way < 2 else mine
        if way == 0:
            source, there = wide.at[p, :, planes : planes + UNDER, :n, :], wide.at[p, :, under, :n, :]
            return remote(source, there, fwd_s.at[p, 0, 1], fwd_r.at[p, 1, 0], slab=above)
        planes_ = slice(0, fore) if way == 1 else slice(fore, REACH)
        source = wide.at[p, :, UNDER + planes_.start : UNDER + planes_.stop, :n, :]
        there = wide.at[p, :, UNDER + planes + planes_.start : UNDER + planes + planes_.stop, :n, :]
        return remote(source, there, fwd_s.at[p, way - 1, 3 - way], fwd_r.at[p, 1, way], slab=below)

    def orb_spread(p):
        u = 2 * p + c
        sized(z, lambda rows: when(down, lambda: orb_halo(p, 1, rows).start()))
        sized(z, lambda rows: when(up, lambda: orb_halo(p, 0, rows).start()))
        sized(z, lambda rows: orb_mate(u, rows).start())
        par_mate(p, u).start()

    def tri_spread(p, h):
        if h == 0:
            sized(z, lambda rows: when(down, lambda: tri_halo(p, 1, rows).start()))
            sized(z, lambda rows: when(up & flip, lambda: tri_halo(p, 0, rows).start()))
        else:
            if fore < REACH:
                when(down, lambda: tri_halo(p, 2, mine).start())
            sized(z, lambda rows: when(up & jnp.logical_not(flip), lambda: tri_halo(p, 0, rows).start()))
        tri_mate(p, h).start()

    for p in peers:
        sized(p, lambda rows: orb_out(p, rows).start())
        par_out(p).start()
    orb_spread(z)
    for j in range(1, nf):
        freq_copy(j).start()
    when(up, lambda: pot_halo(0).start())
    when(down, lambda: pot_halo(1).start())
    units = [(n, h) for n in range(chips - 1) for h in range(PIECES)]
    for n, h in units:
        sized(peers[n], lambda rows: tri_out(peers[n], h, rows).start())

    for p in froms:
        sized(z, lambda rows: orb_in(p, rows).wait_recv())
        par_mate(p, 2 * p + c).wait_recv()
        orb_spread(p)
    sized(z, lambda rows: own_tri(rows).wait())
    for h in range(PIECES):
        tri_spread(z, h)
    for p in [z] + froms:

        def pass_on(rows):
            def side(way):
                halo_mate(2 * p + c, way, rows).wait_recv()
                halo_mate(2 * p + c, way, rows).start()

            when(up, lambda: side(1))
            when(down, lambda: side(0))

        sized(z, pass_on)

    for copy in locals_[3:]:
        copy.wait()
    for j in range(1, nf):
        freq_copy(j).wait_recv()
    for j in range(chips):
        u = 2 * j + 1 - c

        def waits(rows):
            orb_mate(u, rows).wait_recv()
            when(up, lambda: halo_mate(u, 1, rows).wait_recv())
            when(down, lambda: halo_mate(u, 0, rows).wait_recv())

        sized(z, waits)
        par_mate(j, u).wait_recv()
    if near:
        for j in range(1, nf):
            pl.semaphore_signal(gate, inc=1, device_id={"freq": lax.rem(f + j, nf)}, device_id_type=MESH)
    when(up, lambda: pot_halo(1).wait_recv())
    when(down, lambda: pot_halo(0).wait_recv())

    inverse = 1.0 / 4.5
    hop = -0.5 / 4.5

    for i in range(norb):
        energy = pars[i]
        terms = [0.0, 0.0, 0.0, 0.0]
        for w in range(nf):
            mu = (energy + freqs[w, 4:5, :]) * inverse
            c0, c1, c2, c3 = (freqs[w, n : 1 + n, :] for n in range(4))
            b0, b1, b2, b3 = c0 - c2, c1 - 3.0 * c3, 2.0 * c2, 4.0 * c3
            terms[0] += b0 - mu * (b1 - mu * (b2 - mu * b3))
            terms[1] += b1 - mu * (2.0 * b2 - 3.0 * mu * b3)
            terms[2] += b2 - 3.0 * mu * b3
            terms[3] += b3
        for n in range(4):
            weights[n, i] = jnp.broadcast_to(terms[n], (8, nz))

    lane = lax.broadcasted_iota(jnp.int32, (mine, nz), 1)
    rows_ = lax.broadcasted_iota(jnp.int32, (mine, nz), 0) + y_mine

    def links(position, size):
        return (position >= 1).astype(jnp.float32) + (position + 1 < size).astype(jnp.float32)

    def coef_plane(x, carry):
        column = jnp.zeros((mine, nz), jnp.int32) + (s * planes + x)
        for dz in range(-REACH, REACH + 1):
            group = [(n, off) for n, off in enumerate(OFFSETS) if off[2] == dz]
            if not group:
                continue
            depth = lane - dz
            inside = ((depth >= 0) & (depth < nz)).astype(jnp.float32)
            least = min(sum(map(abs, off)) for _, off in group)
            scaled = {}
            for i in range(norb):
                centre = rolled(orbs[i, UNDER + x, :mine, :], dz) * inside
                for n in range(least, 4):
                    scaled[n, i] = weights[n, i, :mine, :] * centre

            def local(a, b, e):
                return rolled(pots[2 + x + a, pl.ds(8 + y_mine + b, mine), :], dz - e) * inverse

            for index, (dx, dy, _) in group:
                steps = abs(dx) + abs(dy) + abs(dz)
                sums = {n: 0.0 for n in range(steps, 4)}
                for i in range(norb):
                    there = orbs[i, UNDER + x + dx, dy : dy + mine, :]
                    for n in sums:
                        sums[n] = sums[n] + scaled[n, i] * there
                if steps == 3:
                    kind = tuple(sorted(map(abs, (dx, dy, dz))))
                    coef = (PATHS[kind] * hop**3) * sums[3]
                elif steps == 2:
                    here, end = local(0, 0, 0), local(dx, dy, dz)
                    corners = [p for p in ((dx, 0, 0), (0, dy, 0), (0, 0, dz)) if p != (0, 0, 0)]
                    if len(corners) == 1:
                        middle = local(int(dx / 2), int(dy / 2), int(dz / 2))
                        coef = hop**2 * (sums[2] + (here + middle + end) * sums[3])
                    else:
                        middle = local(*corners[0]) + local(*corners[1])
                        coef = hop**2 * (2.0 * sums[2] + (2.0 * (here + end) + middle) * sums[3])
                elif steps == 1:
                    here, end = local(0, 0, 0), local(dx, dy, dz)
                    place = (column, rows_, depth)
                    size = (planes * ns, ny, nz)
                    move = (dx, dy, dz)
                    side, along = 0.0, 0.0
                    for axis in range(3):
                        if move[axis]:
                            along = links(place[axis], size[axis]) + links(place[axis] + move[axis], size[axis])
                        else:
                            side = side + links(place[axis], size[axis])
                    walks = along + 3.0 * side - 1.0
                    cubic = here * here + here * end + end * end + hop**2 * walks
                    coef = hop * (sums[1] + (here + end) * sums[2] + cubic * sums[3])
                else:
                    here = local(0, 0, 0)
                    degree = links(column, planes * ns) + links(rows_, ny) + links(lane, nz)
                    beside = local(1, 0, 0) + local(-1, 0, 0) + local(0, 1, 0) + local(0, -1, 0)
                    beside = beside + jnp.where(lane + 1 < nz, local(0, 0, 1), 0.0)
                    beside = beside + jnp.where(lane >= 1, local(0, 0, -1), 0.0)
                    square = here * here + hop**2 * degree
                    cube = here * (here * here + 2.0 * hop**2 * degree) + hop**2 * beside
                    coef = 0.5 * (sums[0] + here * sums[1] + square * sums[2] + cube * sums[3])
                coefs[x, index] = coef
        return carry

    lax.fori_loop(0, planes, coef_plane, 0)

    def density(p):
        def halos(rows):
            when(up, lambda: tri_halo(p, 1, rows).wait_recv())
            when(down, lambda: tri_halo(p, 0, rows).wait_recv())

        sized(z, halos)
        if fore < REACH:
            when(up, lambda: tri_halo(p, 2, mine).wait_recv())

        def plane_step(x, carry):
            sums_ = [0.0] * per
            for dz in range(-REACH, REACH + 1):
                group = [(n, off) for n, off in enumerate(OFFSETS) if off[2] == dz]
                if not group:
                    continue
                sums = [0.0] * per
                for index, (dx, dy, _) in group:
                    coef = coefs[x, index]
                    for k in range(per):
                        sums[k] = sums[k] + coef * wide[p, k, UNDER + x + dx, dy : dy + mine, :]
                for k in range(per):
                    sums_[k] = sums_[k] + rolled(sums[k], -dz)
            for k in range(per):
                dens[p, k, x] = sums_[k]
            return carry

        lax.fori_loop(0, planes, plane_step, 0)

    def take(n, h):
        sized(z, lambda rows: tri_in(froms[n], h, rows).wait_recv())
        tri_spread(froms[n], h)

    contract = (((1,), (1,)), ((), ()))
    part_ = chips * per

    def gram_of(blocks):
        width = len(blocks) * per

        def gram_plane(x, acc):
            for r in range(mine):
                ours = wide[:, :, UNDER + x, r, :].reshape(part_, nz)
                theirs = other[:, :, x, r, :].reshape(part_, nz)
                right = jnp.concatenate([dens[p, :, x, r, :] for p in blocks], axis=0)
                acc = acc + lax.dot_general(
                    jnp.concatenate([ours, theirs], axis=0), right, contract,
                    precision=lax.Precision.HIGH, preferred_element_type=jnp.float32,
                )
            return acc

        return lax.fori_loop(0, planes, gram_plane, jnp.zeros((total, width), jnp.float32))

    work = [z] + [froms[n] for n, h in units if h == PIECES - 1]
    done = 0
    for step, (n, h) in enumerate(units):
        take(n, h)
        if h == PIECES - 1:
            density(work[done])
            done += 1
    for j in range(chips):
        for h in range(PIECES):
            tri_mate(j, h).wait_recv()
    early = gram_of(work[:-1])
    density(work[-1])
    late = gram_of(work[-1:])
    gram = jnp.concatenate([early, late], axis=1)
    index = lax.broadcasted_iota(jnp.int32, (total, total), 0)
    far = index // part_
    place = lax.rem(index, part_)
    trial = (2 * (place // per) + c + far * (1 - 2 * c)) * per + lax.rem(place, per)
    pick = (picks[...] == trial).astype(jnp.float32)
    slot = lax.broadcasted_iota(jnp.int32, (part_, total), 0)
    chip = jnp.zeros((part_, total), jnp.int32)
    for n, p in enumerate(work):
        chip = jnp.where(slot // per == n, p, chip)
    chosen = (picks[...] == (2 * chip + c) * per + lax.rem(slot, per)).astype(jnp.float32)
    factor = 1.0 / jnp.sqrt(jnp.float32(planes * ns * ny * nz * norb))
    moved = lax.dot_general(
        pick, gram * factor, (((0,), (0,)), ((), ())), precision=HIGH, preferred_element_type=jnp.float32
    )
    final = jnp.dot(moved, chosen, precision=HIGH, preferred_element_type=jnp.float32)
    final = final + final.T
    owned = total // (nt * ns)
    for r in range(nt * ns):
        rows_out[r] = final[r * owned : (r + 1) * owned]
    if near:
        for j in range(1, nf):
            pl.semaphore_wait(gate, 1)

    def me():
        return (t * ns + s) * nf + f

    def row_copy(k):
        pt, ps, pf = device(k)
        return remote(
            rows_out.at[pt * ns + ps], rows_in.at[me()], row_s.at[k], row_r.at[k], trial=pt, slab=ps, freq=pf
        )

    def each(action):
        if count <= 64:
            for k in range(1, count):
                action(k)
        else:
            pl.loop(1, count)(action)

    each(lambda k: row_copy(k).start())
    rows_in[me()] = rows_out[t * ns + s]
    for j in range(1, nf):
        freq_copy(j).wait_send()
    when(up, lambda: pot_halo(0).wait_send())
    when(down, lambda: pot_halo(1).wait_send())
    for n, p in enumerate(peers):
        par_out(p).wait_send()

        def out_waits(rows):
            orb_out(p, rows).wait_send()
            for h in range(PIECES):
                tri_out(p, h, rows).wait_send()

        sized(p, out_waits)

    def sends(rows):
        for p in range(chips):
            u = 2 * p + c
            orb_mate(u, rows).wait_send()

            @pl.when(up)
            def _():
                orb_halo(p, 0, rows).wait_send()
                halo_mate(u, 1, rows).wait_send()
                tri_halo(p, 0, rows).wait_send()

            @pl.when(down)
            def _():
                orb_halo(p, 1, rows).wait_send()
                halo_mate(u, 0, rows).wait_send()
                tri_halo(p, 1, rows).wait_send()

    sized(z, sends)
    for p in range(chips):
        par_mate(p, 2 * p + c).wait_send()
        if fore < REACH:
            when(down, lambda: tri_halo(p, 2, mine).wait_send())
        for h in range(PIECES):
            tri_mate(p, h).wait_send()
    each(lambda k: row_copy(k).wait())
    out[...] = jnp.sum(rows_in[...], axis=0)


def local(sizes, orbitals, energies, potential, trials, cheb, shifts, column_order):
    nt, ns, nf = sizes
    per, planes, ny, nz = trials.shape
    norb = orbitals.shape[0] * nt
    chips = nt // 2
    mine = ny // nf // chips
    tall = -(-(mine + REACH) // 8) * 8
    deep = planes + UNDER + REACH
    total = nt * per
    owned = total // (nt * ns)
    count = nt * ns * nf
    f32 = jnp.float32
    dma = pltpu.SemaphoreType.DMA
    anywhere = pl.BlockSpec(memory_space=pltpu.HBM)
    return pl.pallas_call(
        functools.partial(kernel, sizes),
        out_shape=jax.ShapeDtypeStruct((owned, total), f32),
        in_specs=[anywhere] * 7,
        out_specs=pl.BlockSpec(memory_space=pltpu.VMEM),
        scratch_shapes=[
            pltpu.VMEM((norb, deep, tall, nz), f32),
            pltpu.VMEM((chips, per, deep, tall, nz), f32),
            pltpu.VMEM((chips, per, planes, mine, nz), f32),
            pltpu.VMEM((planes + 4, ny + 16, nz), f32),
            pltpu.VMEM((norb, 8, nz), f32),
            pltpu.VMEM((nf, 8, nz), f32),
            pltpu.VMEM((4, norb, 8, nz), f32),
            pltpu.VMEM((planes, len(OFFSETS), mine, nz), f32),
            pltpu.VMEM((chips, per, planes, mine, nz), f32),
            pltpu.VMEM((nt * ns, owned, total), f32),
            pltpu.VMEM((count, owned, total), f32),
            pltpu.SMEM((1,), f32),
            pltpu.SMEM((1, 4), f32),
            pltpu.SMEM((1,), f32),
            pltpu.VMEM((1, total), jnp.int32),
            dma((chips, 6)), dma((nt, 3)), dma((2 * chips,)), dma((nt,)),
            dma((2,)), dma((2,)), dma((nf,)), dma((nf,)),
            dma((chips, PIECES)), dma((chips, PIECES)), dma((chips, PIECES, 3)), dma((chips, PIECES, 3)),
            dma((count,)), dma((count,)),
            dma((7,)),
            pltpu.SemaphoreType.REGULAR,
        ],
        compiler_params=pltpu.CompilerParams(
            collective_id=0, has_side_effects=True, vmem_limit_bytes=67043328 - 65536
        ),
    )(orbitals, energies, potential, trials, cheb, shifts, column_order[None])


def solution(mesh):
    sizes = tuple(mesh.shape[name] for name in ("trial", "slab", "freq"))
    in_specs = (
        P("trial", "slab", None, None),
        P("trial"),
        P("slab", None, None),
        P("trial", "slab", None, None),
        P("freq", None),
        P("freq"),
        P(),
    )
    out_specs = P(("trial", "slab"), None)
    return jax.shard_map(
        functools.partial(local, sizes), mesh=mesh, in_specs=in_specs, out_specs=out_specs, check_vma=False
    )
```

```python
import functools

import jax
import jax.numpy as jnp
from jax import lax
from jax.experimental import pallas as pl
from jax.experimental.pallas import tpu as pltpu
from jax.sharding import PartitionSpec as P

REACH = 3
UNDER = 2
MESH = pl.DeviceIdType.MESH
HIGH = lax.Precision.HIGHEST

OFFSETS = [
    (dx, dy, dz)
    for dz in range(-REACH, REACH + 1)
    for dx in range(-REACH, REACH + 1)
    for dy in range(REACH + 1)
    if abs(dx) + abs(dy) + abs(dz) <= REACH and (dy, dx, dz) >= (0, 0, 0)
]
PATHS = {(1, 1, 1): 6.0, (0, 1, 2): 3.0, (0, 0, 3): 1.0}
PIECES = 2


def rolled(value, shift):
    shift = shift % value.shape[1]
    return value if shift == 0 else pltpu.roll(value, shift, 1)


def when(condition, action):
    pl.when(condition)(action)


def kernel(
    sizes, orb, ene, pot, tri, che, shi, order, out,
    orbs, wide, other, pots, pars, freqs, weights, coefs, dens, t_high, t_low, d_both, rows_out, rows_in,
    ene_m, che_m, shi_m, picks,
    orb_s, orb_r, par_s, par_r, pot_s, pot_r, frq_s, frq_r,
    tri_s, tri_r, fwd_s, fwd_r, row_s, row_r, loc, gate,
):
    nt, ns, nf = sizes
    per, planes, ny, nz = tri.shape
    norb = orbs.shape[0]
    half = ny // nf
    total = nt * per
    chips = nt // 2
    mine = half // chips
    tall = mine + REACH
    sizes_ = (min(REACH, planes - 1), planes - min(REACH, planes - 1))
    deep = planes + UNDER + REACH
    t, s, f = lax.axis_index("trial"), lax.axis_index("slab"), lax.axis_index("freq")
    z, c = t // 2, lax.rem(t, 2)
    mate = t + 1 - 2 * c
    first, last = s == 0, s == ns - 1
    up, down = s < ns - 1, s > 0
    inner = slice(UNDER, UNDER + planes)
    over, under = slice(UNDER + planes, deep), slice(0, UNDER)
    near = ns <= 2 and nf <= 2
    y_mine = f * half + z * mine

    def beyond(zz):
        return (f == nf - 1) & (zz == chips - 1)

    def sized(zz, action):
        when(beyond(zz), lambda: action(mine))
        when(jnp.logical_not(beyond(zz)), lambda: action(tall))

    wrows = min(mine + 16, ny)
    y_pot = jnp.clip(y_mine - 8, 0, ny - wrows)
    win = pl.ds(y_pot, wrows)
    win_to = pl.ds(y_pot + 8, wrows)

    def own_orb(rows):
        return pltpu.make_async_copy(orb.at[0, :, pl.ds(y_mine, rows), :], orbs.at[t, inner, :rows, :], loc.at[0])

    def own_tri(rows):
        return pltpu.make_async_copy(tri.at[:, :, pl.ds(y_mine, rows), :], wide.at[z, :, inner, :rows, :], loc.at[1])

    locals_ = [
        pltpu.make_async_copy(ene, ene_m, loc.at[2]),
        pltpu.make_async_copy(che, che_m, loc.at[3]),
        pltpu.make_async_copy(shi, shi_m, loc.at[4]),
        pltpu.make_async_copy(pot.at[:, win, :], pots.at[2 : planes + 2, win_to, :], loc.at[5]),
        pltpu.make_async_copy(order, picks, loc.at[6]),
    ]
    def device(k):
        dt, ds, df = k // (ns * nf), (k // nf) % ns, k % nf
        return lax.rem(t + dt, nt), lax.rem(s + ds, ns), lax.rem(f + df, nf)

    count = nt * ns * nf
    barrier = pltpu.get_barrier_semaphore()
    below, above = jnp.maximum(s - 1, 0), jnp.minimum(s + 1, ns - 1)
    near_z = z + 1 - 2 * lax.rem(z, 2)
    if chips == 4:
        two, three = lax.rem(z + 2, chips), lax.rem(near_z + 2, chips)
        peers = [near_z, two, three]
        froms = [near_z, two, three]
    else:
        peers = [lax.rem(z + k, chips) for k in range(1, chips)]
        froms = [lax.rem(z + chips - k, chips) for k in range(1, chips)]

    def greet(**where):
        pl.semaphore_signal(barrier, inc=1, device_id=where, device_id_type=MESH)

    if near:
        for p in peers:
            greet(trial=2 * p + c)
        greet(trial=mate)
        for j in range(1, ns):
            greet(slab=lax.rem(s + j, ns))
        for j in range(1, nf):
            greet(freq=lax.rem(f + j, nf))
        greeted = chips + ns + nf - 2
    else:

        @pl.loop(1, count)
        def _(k):
            pt, ps, pf = device(k)
            greet(trial=pt, slab=ps, freq=pf)

        greeted = count - 1

    for copy in locals_[:3]:
        copy.start()
    sized(z, lambda rows: own_orb(rows).start())
    for copy in locals_[3:]:
        copy.start()
    sized(z, lambda rows: own_tri(rows).start())

    pots[:, 0:8, :] = jnp.zeros((planes + 4, 8, nz), jnp.float32)
    pots[:, ny + 8 :, :] = jnp.zeros((planes + 4, 8, nz), jnp.float32)

    @pl.when(last)
    def _():
        orbs[:, over] = jnp.zeros((norb, REACH) + orbs.shape[2:], jnp.float32)
        wide[:, :, over] = jnp.zeros((chips, per, REACH) + wide.shape[3:], jnp.float32)
        pots[planes + 2 :] = jnp.zeros((2,) + pots.shape[1:], jnp.float32)

    @pl.when(first)
    def _():
        orbs[:, under] = jnp.zeros((norb, UNDER) + orbs.shape[2:], jnp.float32)
        wide[:, :, under] = jnp.zeros((chips, per, UNDER) + wide.shape[3:], jnp.float32)
        pots[:2] = jnp.zeros((2,) + pots.shape[1:], jnp.float32)

    @pl.when(beyond(z))
    def _():
        orbs[:, :, mine:tall, :] = jnp.zeros((norb, deep, REACH, nz), jnp.float32)
        wide[:, :, :, mine:tall, :] = jnp.zeros((chips, per, deep, REACH, nz), jnp.float32)

    for copy in locals_[:3]:
        copy.wait()
    pars[t] = jnp.full((8, nz), ene_m[0], jnp.float32)
    row = lax.broadcasted_iota(jnp.int32, (8, nz), 0)
    tile = jnp.full((8, nz), shi_m[0], jnp.float32)
    for n in range(4):
        tile = jnp.where(row == n, che_m[0, n], tile)
    freqs[f] = tile
    sized(z, lambda rows: own_orb(rows).wait())

    pl.semaphore_wait(barrier, greeted)

    def remote(src, dst, send, recv, **where):
        return pltpu.make_async_remote_copy(
            src_ref=src, dst_ref=dst, send_sem=send, recv_sem=recv, device_id=where, device_id_type=MESH
        )

    def rows_at(p, rows):
        return pl.ds(f * half + p * mine, rows)

    def orb_out(p, rows):
        source = orb.at[0, :, rows_at(p, rows), :]
        return remote(source, orbs.at[t, inner, :rows, :], orb_s.at[p, 0], orb_r.at[t, 0], trial=2 * p + c)

    def orb_in(p, rows):
        block = orbs.at[2 * p + c, inner, :rows, :]
        return remote(block, block, orb_s.at[p, 0], orb_r.at[2 * p + c, 0], trial=mate)

    def orb_mate(u, rows):
        block = orbs.at[u, inner, :rows, :]
        return remote(block, block, orb_s.at[u // 2, 1], orb_r.at[u, 0], trial=mate)

    def short(rows):
        return min(rows, mine + 2)

    def orb_halo(p, way, rows):
        u = 2 * p + c
        n = short(rows)
        if way == 0:
            source, there = orbs.at[u, planes : planes + UNDER, :n, :], orbs.at[u, under, :n, :]
            return remote(source, there, orb_s.at[p, 2], orb_r.at[u, 1], slab=above)
        source, there = orbs.at[u, UNDER : UNDER + REACH, :n, :], orbs.at[u, over, :n, :]
        return remote(source, there, orb_s.at[p, 3], orb_r.at[u, 2], slab=below)

    def halo_mate(u, way, rows):
        block = orbs.at[u, under if way == 0 else over, : short(rows), :]
        return remote(block, block, orb_s.at[u // 2, 4 + way], orb_r.at[u, 1 + way], trial=mate)

    def par_out(p):
        return remote(pars.at[t], pars.at[t], par_s.at[p], par_r.at[t], trial=2 * p + c)

    def par_mate(p, u):
        return remote(pars.at[u], pars.at[u], par_s.at[chips + p], par_r.at[u], trial=mate)

    def pot_halo(way):
        if way == 0:
            source, there = pot.at[planes - 2 :, win, :], pots.at[:2, win_to, :]
            return remote(source, there, pot_s.at[0], pot_r.at[0], slab=above)
        source, there = pot.at[:2, win, :], pots.at[planes + 2 :, win_to, :]
        return remote(source, there, pot_s.at[1], pot_r.at[1], slab=below)

    def freq_copy(j):
        return remote(freqs.at[f], freqs.at[f], frq_s.at[j], frq_r.at[j], freq=lax.rem(f + j, nf))

    flip = first & (ns > 1)

    def start(h):
        return jnp.where(flip, sizes_[1], 0) if h == 0 else jnp.where(flip, 0, sizes_[0])

    def held(h):
        return pl.ds(UNDER + start(h), sizes_[h])

    def tri_out(p, h, rows):
        source = tri.at[:, pl.ds(start(h), sizes_[h]), rows_at(p, rows), :]
        there = wide.at[z, :, held(h), :rows, :]
        return remote(source, there, tri_s.at[p, h], tri_r.at[z, h], trial=2 * p + c)

    def tri_in(p, h, rows):
        block = wide.at[p, :, held(h), :rows, :]
        return remote(block, block, tri_s.at[p, h], tri_r.at[p, h], trial=mate)

    def tri_mate(p, h):
        source = wide.at[p, :, held(h), :mine, :]
        there = other.at[p, :, pl.ds(start(h), sizes_[h])]
        return remote(source, there, fwd_s.at[p, h], fwd_r.at[p, h], trial=mate)

    def tri_halo(p, way, rows):
        n = short(rows)
        if way == 0:
            source, there = wide.at[p, :, planes : planes + UNDER, :n, :], wide.at[p, :, under, :n, :]
            return remote(source, there, fwd_s.at[p, 2], fwd_r.at[p, 2], slab=above)
        source, there = wide.at[p, :, UNDER : UNDER + REACH, :n, :], wide.at[p, :, over, :n, :]
        return remote(source, there, fwd_s.at[p, 3], fwd_r.at[p, 3], slab=below)

    def orb_spread(p):
        u = 2 * p + c
        sized(z, lambda rows: when(down, lambda: orb_halo(p, 1, rows).start()))
        sized(z, lambda rows: when(up, lambda: orb_halo(p, 0, rows).start()))
        sized(z, lambda rows: orb_mate(u, rows).start())
        par_mate(p, u).start()

    def tri_spread(p, h):
        if h == 0:
            sized(z, lambda rows: when(down, lambda: tri_halo(p, 1, rows).start()))
            sized(z, lambda rows: when(up & flip, lambda: tri_halo(p, 0, rows).start()))
        else:
            sized(z, lambda rows: when(up & jnp.logical_not(flip), lambda: tri_halo(p, 0, rows).start()))
        tri_mate(p, h).start()

    for p in peers:
        sized(p, lambda rows: orb_out(p, rows).start())
        par_out(p).start()
    orb_spread(z)
    for j in range(1, nf):
        freq_copy(j).start()
    when(up, lambda: pot_halo(0).start())
    when(down, lambda: pot_halo(1).start())
    for n in range(chips - 1):
        for h in range(PIECES):
            sized(peers[n], lambda rows: tri_out(peers[n], h, rows).start())

    for p in froms:
        sized(z, lambda rows: orb_in(p, rows).wait_recv())
        par_mate(p, 2 * p + c).wait_recv()
        orb_spread(p)
    sized(z, lambda rows: own_tri(rows).wait())
    for h in range(PIECES):
        tri_spread(z, h)
    for p in [z] + froms:

        def pass_on(rows):
            def side(way):
                halo_mate(2 * p + c, way, rows).wait_recv()
                halo_mate(2 * p + c, way, rows).start()

            when(up, lambda: side(1))
            when(down, lambda: side(0))

        sized(z, pass_on)

    for copy in locals_[3:]:
        copy.wait()
    for j in range(1, nf):
        freq_copy(j).wait_recv()
    for j in range(chips):
        u = 2 * j + 1 - c

        def waits(rows):
            orb_mate(u, rows).wait_recv()
            when(up, lambda: halo_mate(u, 1, rows).wait_recv())
            when(down, lambda: halo_mate(u, 0, rows).wait_recv())

        sized(z, waits)
        par_mate(j, u).wait_recv()
    if near:
        for j in range(1, nf):
            pl.semaphore_signal(gate, inc=1, device_id={"freq": lax.rem(f + j, nf)}, device_id_type=MESH)
    when(up, lambda: pot_halo(1).wait_recv())
    when(down, lambda: pot_halo(0).wait_recv())

    inverse = 1.0 / 4.5
    hop = -0.5 / 4.5

    for i in range(norb):
        energy = pars[i]
        terms = [0.0, 0.0, 0.0, 0.0]
        for w in range(nf):
            mu = (energy + freqs[w, 4:5, :]) * inverse
            c0, c1, c2, c3 = (freqs[w, n : 1 + n, :] for n in range(4))
            b0, b1, b2, b3 = c0 - c2, c1 - 3.0 * c3, 2.0 * c2, 4.0 * c3
            terms[0] += b0 - mu * (b1 - mu * (b2 - mu * b3))
            terms[1] += b1 - mu * (2.0 * b2 - 3.0 * mu * b3)
            terms[2] += b2 - 3.0 * mu * b3
            terms[3] += b3
        for n in range(4):
            weights[n, i] = jnp.broadcast_to(terms[n], (8, nz))

    lane = lax.broadcasted_iota(jnp.int32, (mine, nz), 1)
    rows_ = lax.broadcasted_iota(jnp.int32, (mine, nz), 0) + y_mine

    def links(position, size):
        return (position >= 1).astype(jnp.float32) + (position + 1 < size).astype(jnp.float32)

    def coef_plane(x, carry):
        column = jnp.zeros((mine, nz), jnp.int32) + (s * planes + x)
        for dz in range(-REACH, REACH + 1):
            group = [(n, off) for n, off in enumerate(OFFSETS) if off[2] == dz]
            if not group:
                continue
            depth = lane - dz
            inside = ((depth >= 0) & (depth < nz)).astype(jnp.float32)
            least = min(sum(map(abs, off)) for _, off in group)
            scaled = {}
            for i in range(norb):
                centre = rolled(orbs[i, UNDER + x, :mine, :], dz) * inside
                for n in range(least, 4):
                    scaled[n, i] = weights[n, i, :mine, :] * centre

            def local(a, b, e):
                return rolled(pots[2 + x + a, pl.ds(8 + y_mine + b, mine), :], dz - e) * inverse

            for index, (dx, dy, _) in group:
                steps = abs(dx) + abs(dy) + abs(dz)
                sums = {n: 0.0 for n in range(steps, 4)}
                for i in range(norb):
                    there = orbs[i, UNDER + x + dx, dy : dy + mine, :]
                    for n in sums:
                        sums[n] = sums[n] + scaled[n, i] * there
                if steps == 3:
                    kind = tuple(sorted(map(abs, (dx, dy, dz))))
                    coef = (PATHS[kind] * hop**3) * sums[3]
                elif steps == 2:
                    here, end = local(0, 0, 0), local(dx, dy, dz)
                    corners = [p for p in ((dx, 0, 0), (0, dy, 0), (0, 0, dz)) if p != (0, 0, 0)]
                    if len(corners) == 1:
                        middle = local(int(dx / 2), int(dy / 2), int(dz / 2))
                        coef = hop**2 * (sums[2] + (here + middle + end) * sums[3])
                    else:
                        middle = local(*corners[0]) + local(*corners[1])
                        coef = hop**2 * (2.0 * sums[2] + (2.0 * (here + end) + middle) * sums[3])
                elif steps == 1:
                    here, end = local(0, 0, 0), local(dx, dy, dz)
                    place = (column, rows_, depth)
                    size = (planes * ns, ny, nz)
                    move = (dx, dy, dz)
                    side, along = 0.0, 0.0
                    for axis in range(3):
                        if move[axis]:
                            along = links(place[axis], size[axis]) + links(place[axis] + move[axis], size[axis])
                        else:
                            side = side + links(place[axis], size[axis])
                    walks = along + 3.0 * side - 1.0
                    cubic = here * here + here * end + end * end + hop**2 * walks
                    coef = hop * (sums[1] + (here + end) * sums[2] + cubic * sums[3])
                else:
                    here = local(0, 0, 0)
                    degree = links(column, planes * ns) + links(rows_, ny) + links(lane, nz)
                    beside = local(1, 0, 0) + local(-1, 0, 0) + local(0, 1, 0) + local(0, -1, 0)
                    beside = beside + jnp.where(lane + 1 < nz, local(0, 0, 1), 0.0)
                    beside = beside + jnp.where(lane >= 1, local(0, 0, -1), 0.0)
                    square = here * here + hop**2 * degree
                    cube = here * (here * here + 2.0 * hop**2 * degree) + hop**2 * beside
                    coef = 0.5 * (sums[0] + here * sums[1] + square * sums[2] + cube * sums[3])
                coefs[x, index] = coef
        return carry

    lax.fori_loop(0, planes, coef_plane, 0)

    def density(p):
        def halos(rows):
            when(up, lambda: tri_halo(p, 1, rows).wait_recv())
            when(down, lambda: tri_halo(p, 0, rows).wait_recv())

        sized(z, halos)

        def plane_step(x, carry):
            sums_ = [0.0] * per
            for dz in range(-REACH, REACH + 1):
                group = [(n, off) for n, off in enumerate(OFFSETS) if off[2] == dz]
                if not group:
                    continue
                sums = [0.0] * per
                for index, (dx, dy, _) in group:
                    coef = coefs[x, index]
                    for k in range(per):
                        sums[k] = sums[k] + coef * wide[p, k, UNDER + x + dx, dy : dy + mine, :]
                for k in range(per):
                    sums_[k] = sums_[k] + rolled(sums[k], -dz)
            for k in range(per):
                dens[p, k, x] = sums_[k]
            return carry

        lax.fori_loop(0, planes, plane_step, 0)

    def take(n, h):
        p = froms[n]
        sized(z, lambda rows: tri_in(p, h, rows).wait_recv())
        tri_spread(p, h)

    contract = (((1,), (1,)), ((), ()))

    work = [z] + froms
    both = 2 * per

    def ready(n, h):
        p = work[n]
        tri_mate(p, h).wait_recv()
        for k in range(sizes_[h]):
            x = start(h) + k
            for r in range(mine):
                value = jnp.concatenate([wide[p, :, UNDER + x, r, :], other[p, :, x, r, :]], axis=0)
                high = value.astype(jnp.bfloat16)
                cut = slice(r * nz, (r + 1) * nz)
                t_high[x, n * both : (n + 1) * both, cut] = high
                t_low[x, n * both : (n + 1) * both, cut] = (value - high.astype(jnp.float32)).astype(jnp.bfloat16)

    def weighed(n):
        p = work[n]

        def plane_step(x, carry):
            for r in range(mine):
                value = dens[p, :, x, r, :]
                high = value.astype(jnp.bfloat16).astype(jnp.float32)
                pair = jnp.concatenate([high, value - high], axis=0)
                d_both[x, n * both : (n + 1) * both, r * nz : (r + 1) * nz] = pair.astype(jnp.bfloat16)
            return carry

        lax.fori_loop(0, planes, plane_step, 0)

    def dots(h, lo, hi):
        acc = jnp.zeros((chips * both, (hi - lo) * both), jnp.float32)
        for k in range(sizes_[h]):
            x = start(h) + k
            right = d_both[x, lo * both : hi * both, :]
            for left in (t_high, t_low):
                acc = acc + lax.dot_general(left[x], right, contract, preferred_element_type=jnp.float32)
        return acc

    for h in range(PIECES):
        take(0, h)
    density(work[0])
    for h in range(PIECES):
        ready(0, h)
    weighed(0)
    for n in range(1, chips - 1):
        take(n, 0)
        density(work[n])
        for h in range(PIECES):
            ready(n, h)
        weighed(n)
        if n == chips - 2:
            ready(chips - 1, 0)
            early = dots(0, 0, chips - 1)
        take(n, 1)
    density(work[-1])
    weighed(chips - 1)
    ready(chips - 1, 1)
    early = early + dots(1, 0, chips - 1)
    late = sum(dots(h, chips - 1, chips) for h in range(PIECES))
    gram = jnp.concatenate([early, late], axis=1)
    index = lax.broadcasted_iota(jnp.int32, (total, total), 0)
    chip = jnp.zeros((total, total), jnp.int32)
    for n, p in enumerate(work):
        chip = jnp.where(index // both == n, p, chip)
    inside = lax.rem(index, per)
    far_core = lax.rem(index // per, 2)
    pick = (picks[...] == (2 * chip + c + far_core * (1 - 2 * c)) * per + inside).astype(jnp.float32)
    chosen = (picks[...] == (2 * chip + c) * per + inside).astype(jnp.float32)
    factor = 1.0 / jnp.sqrt(jnp.float32(planes * ns * ny * nz * norb))
    moved = lax.dot_general(
        pick, gram * factor, (((0,), (0,)), ((), ())), precision=HIGH, preferred_element_type=jnp.float32
    )
    final = jnp.dot(moved, chosen, precision=HIGH, preferred_element_type=jnp.float32)
    final = final + final.T
    owned = total // (nt * ns)
    for r in range(nt * ns):
        rows_out[r] = final[r * owned : (r + 1) * owned]
    if near:
        for j in range(1, nf):
            pl.semaphore_wait(gate, 1)

    def me():
        return (t * ns + s) * nf + f

    def row_copy(k):
        pt, ps, pf = device(k)
        return remote(
            rows_out.at[pt * ns + ps], rows_in.at[me()], row_s.at[0], row_r.at[0], trial=pt, slab=ps, freq=pf
        )

    def each(action):
        if count <= 64:
            for k in range(1, count):
                action(k)
        else:
            pl.loop(1, count)(action)

    each(lambda k: row_copy(k).start())
    rows_in[me()] = rows_out[t * ns + s]
    for j in range(1, nf):
        freq_copy(j).wait_send()
    when(up, lambda: pot_halo(0).wait_send())
    when(down, lambda: pot_halo(1).wait_send())
    for n, p in enumerate(peers):
        par_out(p).wait_send()

        def out_waits(rows):
            for h in range(PIECES):
                tri_out(p, h, rows).wait_send()

        sized(p, lambda rows: orb_out(p, rows).wait_send())
        sized(p, out_waits)

    def sends(rows):
        for p in range(chips):
            u = 2 * p + c
            orb_mate(u, rows).wait_send()

            @pl.when(up)
            def _():
                orb_halo(p, 0, rows).wait_send()
                halo_mate(u, 1, rows).wait_send()
                tri_halo(p, 0, rows).wait_send()

            @pl.when(down)
            def _():
                orb_halo(p, 1, rows).wait_send()
                halo_mate(u, 0, rows).wait_send()
                tri_halo(p, 1, rows).wait_send()

    sized(z, sends)
    for p in range(chips):
        par_mate(p, 2 * p + c).wait_send()
        for h in range(PIECES):
            tri_mate(p, h).wait_send()
    rest = rows_in.at[: count - 1]
    remote(rest, rest, row_s.at[0], row_r.at[0], trial=mate).wait()
    out[...] = jnp.sum(rows_in[...], axis=0)


def local(sizes, orbitals, energies, potential, trials, cheb, shifts, column_order):
    nt, ns, nf = sizes
    per, planes, ny, nz = trials.shape
    norb = orbitals.shape[0] * nt
    chips = nt // 2
    mine = ny // nf // chips
    tall = -(-(mine + REACH) // 8) * 8
    deep = planes + UNDER + REACH
    total = nt * per
    owned = total // (nt * ns)
    count = nt * ns * nf
    f32 = jnp.float32
    dma = pltpu.SemaphoreType.DMA
    anywhere = pl.BlockSpec(memory_space=pltpu.HBM)
    return pl.pallas_call(
        functools.partial(kernel, sizes),
        out_shape=jax.ShapeDtypeStruct((owned, total), f32),
        in_specs=[anywhere] * 7,
        out_specs=pl.BlockSpec(memory_space=pltpu.VMEM),
        scratch_shapes=[
            pltpu.VMEM((norb, deep, tall, nz), f32),
            pltpu.VMEM((chips, per, deep, tall, nz), f32),
            pltpu.VMEM((chips, per, planes, mine, nz), f32),
            pltpu.VMEM((planes + 4, ny + 16, nz), f32),
            pltpu.VMEM((norb, 8, nz), f32),
            pltpu.VMEM((nf, 8, nz), f32),
            pltpu.VMEM((4, norb, 8, nz), f32),
            pltpu.VMEM((planes, len(OFFSETS), mine, nz), f32),
            pltpu.VMEM((chips, per, planes, mine, nz), f32),
            pltpu.VMEM((planes, total, mine * nz), jnp.bfloat16),
            pltpu.VMEM((planes, total, mine * nz), jnp.bfloat16),
            pltpu.VMEM((planes, total, mine * nz), jnp.bfloat16),
            pltpu.VMEM((nt * ns, owned, total), f32),
            pltpu.VMEM((count, owned, total), f32),
            pltpu.SMEM((1,), f32),
            pltpu.SMEM((1, 4), f32),
            pltpu.SMEM((1,), f32),
            pltpu.VMEM((1, total), jnp.int32),
            dma((chips, 6)), dma((nt, 3)), dma((2 * chips,)), dma((nt,)),
            dma((2,)), dma((2,)), dma((nf,)), dma((nf,)),
            dma((chips, PIECES)), dma((chips, PIECES)), dma((chips, 4)), dma((chips, 4)),
            dma((1,)), dma((1,)),
            dma((7,)),
            pltpu.SemaphoreType.REGULAR,
        ],
        compiler_params=pltpu.CompilerParams(
            collective_id=0, has_side_effects=True, vmem_limit_bytes=67043328 - 65536
        ),
    )(orbitals, energies, potential, trials, cheb, shifts, column_order[None])


def solution(mesh):
    sizes = tuple(mesh.shape[name] for name in ("trial", "slab", "freq"))
    in_specs = (
        P("trial", "slab", None, None),
        P("trial"),
        P("slab", None, None),
        P("trial", "slab", None, None),
        P("freq", None),
        P("freq"),
        P(),
    )
    out_specs = P(("trial", "slab"), None)
    return jax.shard_map(
        functools.partial(local, sizes), mesh=mesh, in_specs=in_specs, out_specs=out_specs, check_vma=False
    )
```

```python
import functools

import jax
import jax.numpy as jnp
from jax import lax
from jax.experimental import pallas as pl
from jax.experimental.pallas import tpu as pltpu
from jax.sharding import PartitionSpec as P

REACH = 3
UNDER = 2
MESH = pl.DeviceIdType.MESH

OFFSETS = [
    (dx, dy, dz)
    for dz in range(-REACH, REACH + 1)
    for dx in range(-REACH, REACH + 1)
    for dy in range(REACH + 1)
    if abs(dx) + abs(dy) + abs(dz) <= REACH and (dy, dx, dz) >= (0, 0, 0)
]
PATHS = {(1, 1, 1): 6.0, (0, 1, 2): 3.0, (0, 0, 3): 1.0}
PIECES = 2


def rolled(value, shift):
    shift = shift % value.shape[1]
    return value if shift == 0 else pltpu.roll(value, shift, 1)


def when(condition, action):
    pl.when(condition)(action)


def kernel(
    sizes, orb, ene, pot, tri, che, shi, order, out,
    orbs, wide, other, pots, pars, freqs, weights, coefs, dens, t_high, t_low, d_both, rows_out, rows_in,
    ene_m, che_m, shi_m, picks,
    orb_s, orb_r, par_s, par_r, pot_s, pot_r, frq_s, frq_r,
    tri_s, tri_r, fwd_s, fwd_r, row_s, row_r, loc, gate,
):
    nt, ns, nf = sizes
    per, planes, ny, nz = tri.shape
    norb = orbs.shape[0]
    half = ny // nf
    total = nt * per
    chips = nt // 2
    mine = half // chips
    tall = mine + REACH
    sizes_ = (min(REACH, planes - 1), planes - min(REACH, planes - 1))
    deep = planes + UNDER + REACH
    t, s, f = lax.axis_index("trial"), lax.axis_index("slab"), lax.axis_index("freq")
    z, c = t // 2, lax.rem(t, 2)
    mate = t + 1 - 2 * c
    first, last = s == 0, s == ns - 1
    up, down = s < ns - 1, s > 0
    inner = slice(UNDER, UNDER + planes)
    over, under = slice(UNDER + planes, deep), slice(0, UNDER)
    near = ns <= 2 and nf <= 2
    y_mine = f * half + z * mine

    def beyond(zz):
        return (f == nf - 1) & (zz == chips - 1)

    def sized(zz, action):
        when(beyond(zz), lambda: action(mine))
        when(jnp.logical_not(beyond(zz)), lambda: action(tall))

    wrows = min(mine + 16, ny)
    y_pot = jnp.clip(y_mine - 8, 0, ny - wrows)
    win = pl.ds(y_pot, wrows)
    win_to = pl.ds(y_pot + 8, wrows)

    def own_orb(rows):
        return pltpu.make_async_copy(orb.at[0, :, pl.ds(y_mine, rows), :], orbs.at[t, inner, :rows, :], loc.at[0])

    def own_tri(rows):
        return pltpu.make_async_copy(tri.at[:, :, pl.ds(y_mine, rows), :], wide.at[z, :, inner, :rows, :], loc.at[1])

    locals_ = [
        pltpu.make_async_copy(ene, ene_m, loc.at[2]),
        pltpu.make_async_copy(che, che_m, loc.at[3]),
        pltpu.make_async_copy(shi, shi_m, loc.at[4]),
        pltpu.make_async_copy(pot.at[:, win, :], pots.at[2 : planes + 2, win_to, :], loc.at[5]),
        pltpu.make_async_copy(order, picks, loc.at[6]),
    ]
    def device(k):
        dt, ds, df = k // (ns * nf), (k // nf) % ns, k % nf
        return lax.rem(t + dt, nt), lax.rem(s + ds, ns), lax.rem(f + df, nf)

    count = nt * ns * nf
    barrier = pltpu.get_barrier_semaphore()
    below, above = jnp.maximum(s - 1, 0), jnp.minimum(s + 1, ns - 1)
    near_z = z + 1 - 2 * lax.rem(z, 2)
    if chips == 4:
        two, three = lax.rem(z + 2, chips), lax.rem(near_z + 2, chips)
        peers = [near_z, two, three]
        froms = [near_z, two, three]
    else:
        peers = [lax.rem(z + k, chips) for k in range(1, chips)]
        froms = [lax.rem(z + chips - k, chips) for k in range(1, chips)]

    def greet(**where):
        pl.semaphore_signal(barrier, inc=1, device_id=where, device_id_type=MESH)

    if near:
        for p in peers:
            greet(trial=2 * p + c)
        greet(trial=mate)
        for j in range(1, ns):
            greet(slab=lax.rem(s + j, ns))
        for j in range(1, nf):
            greet(freq=lax.rem(f + j, nf))
        greeted = chips + ns + nf - 2
    else:

        @pl.loop(1, count)
        def _(k):
            pt, ps, pf = device(k)
            greet(trial=pt, slab=ps, freq=pf)

        greeted = count - 1

    for copy in locals_[:3]:
        copy.start()
    sized(z, lambda rows: own_orb(rows).start())
    for copy in locals_[3:]:
        copy.start()
    sized(z, lambda rows: own_tri(rows).start())

    pots[:, 0:8, :] = jnp.zeros((planes + 4, 8, nz), jnp.float32)
    pots[:, ny + 8 :, :] = jnp.zeros((planes + 4, 8, nz), jnp.float32)

    @pl.when(last)
    def _():
        orbs[:, over] = jnp.zeros((norb, REACH) + orbs.shape[2:], jnp.float32)
        wide[:, :, over] = jnp.zeros((chips, per, REACH) + wide.shape[3:], jnp.float32)
        pots[planes + 2 :] = jnp.zeros((2,) + pots.shape[1:], jnp.float32)

    @pl.when(first)
    def _():
        orbs[:, under] = jnp.zeros((norb, UNDER) + orbs.shape[2:], jnp.float32)
        wide[:, :, under] = jnp.zeros((chips, per, UNDER) + wide.shape[3:], jnp.float32)
        pots[:2] = jnp.zeros((2,) + pots.shape[1:], jnp.float32)

    @pl.when(beyond(z))
    def _():
        orbs[:, :, mine:tall, :] = jnp.zeros((norb, deep, REACH, nz), jnp.float32)
        wide[:, :, :, mine:tall, :] = jnp.zeros((chips, per, deep, REACH, nz), jnp.float32)

    for copy in locals_[:3]:
        copy.wait()
    pars[t] = jnp.full((8, nz), ene_m[0], jnp.float32)
    row = lax.broadcasted_iota(jnp.int32, (8, nz), 0)
    tile = jnp.full((8, nz), shi_m[0], jnp.float32)
    for n in range(4):
        tile = jnp.where(row == n, che_m[0, n], tile)
    freqs[f] = tile
    sized(z, lambda rows: own_orb(rows).wait())

    pl.semaphore_wait(barrier, greeted)

    def remote(src, dst, send, recv, **where):
        return pltpu.make_async_remote_copy(
            src_ref=src, dst_ref=dst, send_sem=send, recv_sem=recv, device_id=where, device_id_type=MESH
        )

    def rows_at(p, rows):
        return pl.ds(f * half + p * mine, rows)

    def orb_out(p, rows):
        source = orb.at[0, :, rows_at(p, rows), :]
        return remote(source, orbs.at[t, inner, :rows, :], orb_s.at[p, 0], orb_r.at[t, 0], trial=2 * p + c)

    def orb_in(p, rows):
        block = orbs.at[2 * p + c, inner, :rows, :]
        return remote(block, block, orb_s.at[p, 0], orb_r.at[2 * p + c, 0], trial=mate)

    def orb_mate(u, rows):
        block = orbs.at[u, inner, :rows, :]
        return remote(block, block, orb_s.at[u // 2, 1], orb_r.at[u, 0], trial=mate)

    def short(rows):
        return min(rows, mine + 2)

    def orb_halo(p, way, rows):
        u = 2 * p + c
        n = short(rows)
        if way == 0:
            source, there = orbs.at[u, planes : planes + UNDER, :n, :], orbs.at[u, under, :n, :]
            return remote(source, there, orb_s.at[p, 2], orb_r.at[u, 1], slab=above)
        source, there = orbs.at[u, UNDER : UNDER + REACH, :n, :], orbs.at[u, over, :n, :]
        return remote(source, there, orb_s.at[p, 3], orb_r.at[u, 2], slab=below)

    def halo_mate(u, way, rows):
        block = orbs.at[u, under if way == 0 else over, : short(rows), :]
        return remote(block, block, orb_s.at[u // 2, 4 + way], orb_r.at[u, 1 + way], trial=mate)

    def par_out(p):
        return remote(pars.at[t], pars.at[t], par_s.at[p], par_r.at[t], trial=2 * p + c)

    def par_mate(p, u):
        return remote(pars.at[u], pars.at[u], par_s.at[chips + p], par_r.at[u], trial=mate)

    def pot_halo(way):
        if way == 0:
            source, there = pot.at[planes - 2 :, win, :], pots.at[:2, win_to, :]
            return remote(source, there, pot_s.at[0], pot_r.at[0], slab=above)
        source, there = pot.at[:2, win, :], pots.at[planes + 2 :, win_to, :]
        return remote(source, there, pot_s.at[1], pot_r.at[1], slab=below)

    def freq_copy(j):
        return remote(freqs.at[f], freqs.at[f], frq_s.at[j], frq_r.at[j], freq=lax.rem(f + j, nf))

    flip = first & (ns > 1)

    def start(h):
        return jnp.where(flip, sizes_[1], 0) if h == 0 else jnp.where(flip, 0, sizes_[0])

    def held(h):
        return pl.ds(UNDER + start(h), sizes_[h])

    def tri_out(p, h, rows):
        source = tri.at[:, pl.ds(start(h), sizes_[h]), rows_at(p, rows), :]
        there = wide.at[z, :, held(h), :rows, :]
        return remote(source, there, tri_s.at[p, h], tri_r.at[z, h], trial=2 * p + c)

    def tri_in(p, h, rows):
        block = wide.at[p, :, held(h), :rows, :]
        return remote(block, block, tri_s.at[p, h], tri_r.at[p, h], trial=mate)

    def tri_mate(p, h):
        source = wide.at[p, :, held(h), :mine, :]
        there = other.at[p, :, pl.ds(start(h), sizes_[h])]
        return remote(source, there, fwd_s.at[p, h], fwd_r.at[p, h], trial=mate)

    def tri_halo(p, way, rows):
        n = short(rows)
        if way == 0:
            source, there = wide.at[p, :, planes : planes + UNDER, :n, :], wide.at[p, :, under, :n, :]
            return remote(source, there, fwd_s.at[p, 2], fwd_r.at[p, 2], slab=above)
        source, there = wide.at[p, :, UNDER : UNDER + REACH, :n, :], wide.at[p, :, over, :n, :]
        return remote(source, there, fwd_s.at[p, 3], fwd_r.at[p, 3], slab=below)

    def orb_spread(p):
        u = 2 * p + c
        sized(z, lambda rows: when(down, lambda: orb_halo(p, 1, rows).start()))
        sized(z, lambda rows: when(up, lambda: orb_halo(p, 0, rows).start()))
        sized(z, lambda rows: orb_mate(u, rows).start())
        par_mate(p, u).start()

    def tri_spread(p, h):
        if h == 0:
            sized(z, lambda rows: when(down, lambda: tri_halo(p, 1, rows).start()))
            sized(z, lambda rows: when(up & flip, lambda: tri_halo(p, 0, rows).start()))
        else:
            sized(z, lambda rows: when(up & jnp.logical_not(flip), lambda: tri_halo(p, 0, rows).start()))
        tri_mate(p, h).start()

    for p in peers:
        sized(p, lambda rows: orb_out(p, rows).start())
        par_out(p).start()
    orb_spread(z)
    for j in range(1, nf):
        freq_copy(j).start()
    when(up, lambda: pot_halo(0).start())
    when(down, lambda: pot_halo(1).start())
    for n, h in [(0, 0), (0, 1)] + [(n, h) for h in range(PIECES) for n in range(1, chips - 1)]:
        sized(peers[n], lambda rows: tri_out(peers[n], h, rows).start())

    for p in froms:
        sized(z, lambda rows: orb_in(p, rows).wait_recv())
        par_mate(p, 2 * p + c).wait_recv()
        orb_spread(p)
    sized(z, lambda rows: own_tri(rows).wait())
    for h in range(PIECES):
        tri_spread(z, h)
    for p in [z] + froms:

        def pass_on(rows):
            def side(way):
                halo_mate(2 * p + c, way, rows).wait_recv()
                halo_mate(2 * p + c, way, rows).start()

            when(up, lambda: side(1))
            when(down, lambda: side(0))

        sized(z, pass_on)

    for copy in locals_[3:]:
        copy.wait()
    for j in range(1, nf):
        freq_copy(j).wait_recv()
    for j in range(chips):
        u = 2 * j + 1 - c

        def waits(rows):
            orb_mate(u, rows).wait_recv()
            when(up, lambda: halo_mate(u, 1, rows).wait_recv())
            when(down, lambda: halo_mate(u, 0, rows).wait_recv())

        sized(z, waits)
        par_mate(j, u).wait_recv()
    if near:
        for j in range(1, nf):
            pl.semaphore_signal(gate, inc=1, device_id={"freq": lax.rem(f + j, nf)}, device_id_type=MESH)
    when(up, lambda: pot_halo(1).wait_recv())
    when(down, lambda: pot_halo(0).wait_recv())

    inverse = 1.0 / 4.5
    hop = -0.5 / 4.5

    for i in range(norb):
        energy = pars[i]
        terms = [0.0, 0.0, 0.0, 0.0]
        for w in range(nf):
            mu = (energy + freqs[w, 4:5, :]) * inverse
            c0, c1, c2, c3 = (freqs[w, n : 1 + n, :] for n in range(4))
            b0, b1, b2, b3 = c0 - c2, c1 - 3.0 * c3, 2.0 * c2, 4.0 * c3
            terms[0] += b0 - mu * (b1 - mu * (b2 - mu * b3))
            terms[1] += b1 - mu * (2.0 * b2 - 3.0 * mu * b3)
            terms[2] += b2 - 3.0 * mu * b3
            terms[3] += b3
        for n in range(4):
            weights[n, i] = jnp.broadcast_to(terms[n], (8, nz))

    lane = lax.broadcasted_iota(jnp.int32, (mine, nz), 1)
    rows_ = lax.broadcasted_iota(jnp.int32, (mine, nz), 0) + y_mine

    def links(position, size):
        return (position >= 1).astype(jnp.float32) + (position + 1 < size).astype(jnp.float32)

    def coef_plane(x, carry):
        column = jnp.zeros((mine, nz), jnp.int32) + (s * planes + x)
        for dz in range(-REACH, REACH + 1):
            group = [(n, off) for n, off in enumerate(OFFSETS) if off[2] == dz]
            if not group:
                continue
            depth = lane - dz
            inside = ((depth >= 0) & (depth < nz)).astype(jnp.float32)
            least = min(sum(map(abs, off)) for _, off in group)
            scaled = {}
            for i in range(norb):
                centre = rolled(orbs[i, UNDER + x, :mine, :], dz) * inside
                for n in range(least, 4):
                    scaled[n, i] = weights[n, i, :mine, :] * centre

            def local(a, b, e):
                return rolled(pots[2 + x + a, pl.ds(8 + y_mine + b, mine), :], dz - e) * inverse

            for index, (dx, dy, _) in group:
                steps = abs(dx) + abs(dy) + abs(dz)
                sums = {n: 0.0 for n in range(steps, 4)}
                for i in range(norb):
                    there = orbs[i, UNDER + x + dx, dy : dy + mine, :]
                    for n in sums:
                        sums[n] = sums[n] + scaled[n, i] * there
                if steps == 3:
                    kind = tuple(sorted(map(abs, (dx, dy, dz))))
                    coef = (PATHS[kind] * hop**3) * sums[3]
                elif steps == 2:
                    here, end = local(0, 0, 0), local(dx, dy, dz)
                    corners = [p for p in ((dx, 0, 0), (0, dy, 0), (0, 0, dz)) if p != (0, 0, 0)]
                    if len(corners) == 1:
                        middle = local(int(dx / 2), int(dy / 2), int(dz / 2))
                        coef = hop**2 * (sums[2] + (here + middle + end) * sums[3])
                    else:
                        middle = local(*corners[0]) + local(*corners[1])
                        coef = hop**2 * (2.0 * sums[2] + (2.0 * (here + end) + middle) * sums[3])
                elif steps == 1:
                    here, end = local(0, 0, 0), local(dx, dy, dz)
                    place = (column, rows_, depth)
                    size = (planes * ns, ny, nz)
                    move = (dx, dy, dz)
                    side, along = 0.0, 0.0
                    for axis in range(3):
                        if move[axis]:
                            along = links(place[axis], size[axis]) + links(place[axis] + move[axis], size[axis])
                        else:
                            side = side + links(place[axis], size[axis])
                    walks = along + 3.0 * side - 1.0
                    cubic = here * here + here * end + end * end + hop**2 * walks
                    coef = hop * (sums[1] + (here + end) * sums[2] + cubic * sums[3])
                else:
                    here = local(0, 0, 0)
                    degree = links(column, planes * ns) + links(rows_, ny) + links(lane, nz)
                    beside = local(1, 0, 0) + local(-1, 0, 0) + local(0, 1, 0) + local(0, -1, 0)
                    beside = beside + jnp.where(lane + 1 < nz, local(0, 0, 1), 0.0)
                    beside = beside + jnp.where(lane >= 1, local(0, 0, -1), 0.0)
                    square = here * here + hop**2 * degree
                    cube = here * (here * here + 2.0 * hop**2 * degree) + hop**2 * beside
                    coef = 0.5 * (sums[0] + here * sums[1] + square * sums[2] + cube * sums[3])
                coefs[x, index] = coef
        return carry

    lax.fori_loop(0, planes, coef_plane, 0)

    def density(p):
        def halos(rows):
            when(up, lambda: tri_halo(p, 1, rows).wait_recv())
            when(down, lambda: tri_halo(p, 0, rows).wait_recv())

        sized(z, halos)

        def plane_step(x, carry):
            sums_ = [0.0] * per
            for dz in range(-REACH, REACH + 1):
                group = [(n, off) for n, off in enumerate(OFFSETS) if off[2] == dz]
                if not group:
                    continue
                sums = [0.0] * per
                for index, (dx, dy, _) in group:
                    coef = coefs[x, index]
                    for k in range(per):
                        sums[k] = sums[k] + coef * wide[p, k, UNDER + x + dx, dy : dy + mine, :]
                for k in range(per):
                    sums_[k] = sums_[k] + rolled(sums[k], -dz)
            for k in range(per):
                dens[p, k, x] = sums_[k]
            return carry

        lax.fori_loop(0, planes, plane_step, 0)

    def take(n, h):
        p = froms[n]
        sized(z, lambda rows: tri_in(p, h, rows).wait_recv())
        tri_spread(p, h)

    contract = (((1,), (1,)), ((), ()))

    work = [z] + froms
    both = 2 * per

    def ready(n, h):
        p = work[n]
        tri_mate(p, h).wait_recv()
        for k in range(sizes_[h]):
            x = start(h) + k
            for r in range(mine):
                value = jnp.concatenate([wide[p, :, UNDER + x, r, :], other[p, :, x, r, :]], axis=0)
                high = value.astype(jnp.bfloat16)
                cut = slice(r * nz, (r + 1) * nz)
                t_high[x, n * both : (n + 1) * both, cut] = high
                t_low[x, n * both : (n + 1) * both, cut] = (value - high.astype(jnp.float32)).astype(jnp.bfloat16)

    def weighed(n):
        p = work[n]

        def plane_step(x, carry):
            for r in range(mine):
                value = dens[p, :, x, r, :]
                high = value.astype(jnp.bfloat16).astype(jnp.float32)
                pair = jnp.concatenate([high, value - high], axis=0)
                d_both[x, n * both : (n + 1) * both, r * nz : (r + 1) * nz] = pair.astype(jnp.bfloat16)
            return carry

        lax.fori_loop(0, planes, plane_step, 0)

    def dots(h, lo, hi):
        acc = jnp.zeros((chips * both, (hi - lo) * both), jnp.float32)
        for k in range(sizes_[h]):
            x = start(h) + k
            right = d_both[x, lo * both : hi * both, :]
            for left in (t_high, t_low):
                acc = acc + lax.dot_general(left[x], right, contract, preferred_element_type=jnp.float32)
        return acc

    for h in range(PIECES):
        take(0, h)
    density(work[0])
    for h in range(PIECES):
        ready(0, h)
    weighed(0)
    take(1, 0)
    density(work[1])
    for h in range(PIECES):
        ready(1, h)
    weighed(1)
    for n in range(2, chips - 1):
        take(n, 0)
    for n in range(2, chips):
        ready(n, 0)
    early = dots(0, 0, 2)
    for n in range(1, chips - 1):
        take(n, 1)
        density(work[n + 1])
        weighed(n + 1)
    for n in range(2, chips):
        ready(n, 1)
    early = early + dots(1, 0, 2)
    late = sum(dots(h, 2, chips) for h in range(PIECES))
    gram = jnp.concatenate([early, late], axis=1)
    index = lax.broadcasted_iota(jnp.int32, (total, total), 0)
    chip = jnp.zeros((total, total), jnp.int32)
    for n, p in enumerate(work):
        chip = jnp.where(index // both == n, p, chip)
    inside = lax.rem(index, per)
    far_core = lax.rem(index // per, 2)
    pick = (picks[...] == (2 * chip + c + far_core * (1 - 2 * c)) * per + inside).astype(jnp.float32)
    chosen = (picks[...] == (2 * chip + c) * per + inside).astype(jnp.float32)
    factor = 1.0 / jnp.sqrt(jnp.float32(planes * ns * ny * nz * norb))
    moved = lax.dot_general(
        pick, gram * factor, (((0,), (0,)), ((), ())), precision=lax.Precision.HIGH, preferred_element_type=jnp.float32
    )
    final = jnp.dot(moved, chosen, precision=lax.Precision.HIGH, preferred_element_type=jnp.float32)
    final = final + final.T
    owned = total // (nt * ns)
    for r in range(nt * ns):
        rows_out[r] = final[r * owned : (r + 1) * owned]
    if near:
        for j in range(1, nf):
            pl.semaphore_wait(gate, 1)

    def me():
        return (t * ns + s) * nf + f

    def row_copy(k):
        pt, ps, pf = device(k)
        return remote(
            rows_out.at[pt * ns + ps], rows_in.at[me()], row_s.at[0], row_r.at[0], trial=pt, slab=ps, freq=pf
        )

    def each(action):
        if count <= 64:
            for k in range(1, count):
                action(k)
        else:
            pl.loop(1, count)(action)

    each(lambda k: row_copy(k).start())
    rows_in[me()] = rows_out[t * ns + s]
    for j in range(1, nf):
        freq_copy(j).wait_send()
    when(up, lambda: pot_halo(0).wait_send())
    when(down, lambda: pot_halo(1).wait_send())
    for n, p in enumerate(peers):
        par_out(p).wait_send()

        def out_waits(rows):
            for h in range(PIECES):
                tri_out(p, h, rows).wait_send()

        sized(p, lambda rows: orb_out(p, rows).wait_send())
        sized(p, out_waits)

    def sends(rows):
        for p in range(chips):
            u = 2 * p + c
            orb_mate(u, rows).wait_send()

            @pl.when(up)
            def _():
                orb_halo(p, 0, rows).wait_send()
                halo_mate(u, 1, rows).wait_send()
                tri_halo(p, 0, rows).wait_send()

            @pl.when(down)
            def _():
                orb_halo(p, 1, rows).wait_send()
                halo_mate(u, 0, rows).wait_send()
                tri_halo(p, 1, rows).wait_send()

    sized(z, sends)
    for p in range(chips):
        par_mate(p, 2 * p + c).wait_send()
        for h in range(PIECES):
            tri_mate(p, h).wait_send()
    rest = rows_in.at[: count - 1]
    remote(rest, rest, row_s.at[0], row_r.at[0], trial=mate).wait()
    out[...] = jnp.sum(rows_in[...], axis=0)


def local(sizes, orbitals, energies, potential, trials, cheb, shifts, column_order):
    nt, ns, nf = sizes
    per, planes, ny, nz = trials.shape
    norb = orbitals.shape[0] * nt
    chips = nt // 2
    mine = ny // nf // chips
    tall = -(-(mine + REACH) // 8) * 8
    deep = planes + UNDER + REACH
    total = nt * per
    owned = total // (nt * ns)
    count = nt * ns * nf
    f32 = jnp.float32
    dma = pltpu.SemaphoreType.DMA
    anywhere = pl.BlockSpec(memory_space=pltpu.HBM)
    return pl.pallas_call(
        functools.partial(kernel, sizes),
        out_shape=jax.ShapeDtypeStruct((owned, total), f32),
        in_specs=[anywhere] * 7,
        out_specs=pl.BlockSpec(memory_space=pltpu.VMEM),
        scratch_shapes=[
            pltpu.VMEM((norb, deep, tall, nz), f32),
            pltpu.VMEM((chips, per, deep, tall, nz), f32),
            pltpu.VMEM((chips, per, planes, mine, nz), f32),
            pltpu.VMEM((planes + 4, ny + 16, nz), f32),
            pltpu.VMEM((norb, 8, nz), f32),
            pltpu.VMEM((nf, 8, nz), f32),
            pltpu.VMEM((4, norb, 8, nz), f32),
            pltpu.VMEM((planes, len(OFFSETS), mine, nz), f32),
            pltpu.VMEM((chips, per, planes, mine, nz), f32),
            pltpu.VMEM((planes, total, mine * nz), jnp.bfloat16),
            pltpu.VMEM((planes, total, mine * nz), jnp.bfloat16),
            pltpu.VMEM((planes, total, mine * nz), jnp.bfloat16),
            pltpu.VMEM((nt * ns, owned, total), f32),
            pltpu.VMEM((count, owned, total), f32),
            pltpu.SMEM((1,), f32),
            pltpu.SMEM((1, 4), f32),
            pltpu.SMEM((1,), f32),
            pltpu.VMEM((1, total), jnp.int32),
            dma((chips, 6)), dma((nt, 3)), dma((2 * chips,)), dma((nt,)),
            dma((2,)), dma((2,)), dma((nf,)), dma((nf,)),
            dma((chips, PIECES)), dma((chips, PIECES)), dma((chips, 4)), dma((chips, 4)),
            dma((1,)), dma((1,)),
            dma((7,)),
            pltpu.SemaphoreType.REGULAR,
        ],
        compiler_params=pltpu.CompilerParams(
            collective_id=0, has_side_effects=True, vmem_limit_bytes=67043328 - 65536
        ),
    )(orbitals, energies, potential, trials, cheb, shifts, column_order[None])


def solution(mesh):
    sizes = tuple(mesh.shape[name] for name in ("trial", "slab", "freq"))
    in_specs = (
        P("trial", "slab", None, None),
        P("trial"),
        P("slab", None, None),
        P("trial", "slab", None, None),
        P("freq", None),
        P("freq"),
        P(),
    )
    out_specs = P(("trial", "slab"), None)
    return jax.shard_map(
        functools.partial(local, sizes), mesh=mesh, in_specs=in_specs, out_specs=out_specs, check_vma=False
    )
```

```python
import functools

import jax
import jax.numpy as jnp
from jax import lax
from jax.experimental import pallas as pl
from jax.experimental.pallas import tpu as pltpu
from jax.sharding import PartitionSpec as P

REACH = 3
UNDER = 2
MESH = pl.DeviceIdType.MESH

OFFSETS = [
    (dx, dy, dz)
    for dz in range(-REACH, REACH + 1)
    for dx in range(-REACH, REACH + 1)
    for dy in range(REACH + 1)
    if abs(dx) + abs(dy) + abs(dz) <= REACH and (dy, dx, dz) >= (0, 0, 0)
]
PATHS = {(1, 1, 1): 6.0, (0, 1, 2): 3.0, (0, 0, 3): 1.0}
PIECES = 2


def rolled(value, shift):
    shift = shift % value.shape[1]
    return value if shift == 0 else pltpu.roll(value, shift, 1)


def when(condition, action):
    pl.when(condition)(action)


def kernel(
    sizes, orb, ene, pot, tri, che, shi, order, out,
    orbs, wide, other, pots, pars, freqs, weights, coefs, dens, t_high, t_low, d_both, rows_out, rows_in,
    ene_m, che_m, shi_m, picks,
    orb_s, orb_r, orb_x, par_s, par_r, par_x, pot_s, pot_r, frq_s, frq_r,
    tri_s, tri_r, fwd_s, fwd_r, row_s, row_r, loc, gate,
):
    nt, ns, nf = sizes
    per, planes, ny, nz = tri.shape
    norb = orbs.shape[0]
    half = ny // nf
    total = nt * per
    chips = nt // 2
    mine = half // chips
    tall = mine + REACH
    sizes_ = (min(REACH, planes - 1), planes - min(REACH, planes - 1))
    deep = planes + UNDER + REACH
    t, s, f = lax.axis_index("trial"), lax.axis_index("slab"), lax.axis_index("freq")
    z, c = t // 2, lax.rem(t, 2)
    mate = t + 1 - 2 * c
    first, last = s == 0, s == ns - 1
    up, down = s < ns - 1, s > 0
    inner = slice(UNDER, UNDER + planes)
    over, under = slice(UNDER + planes, deep), slice(0, UNDER)
    near = ns <= 2 and nf <= 2
    y_mine = f * half + z * mine

    def beyond(zz):
        return (f == nf - 1) & (zz == chips - 1)

    def sized(zz, action):
        when(beyond(zz), lambda: action(mine))
        when(jnp.logical_not(beyond(zz)), lambda: action(tall))

    wrows = min(mine + 16, ny)
    y_pot = jnp.clip(y_mine - 8, 0, ny - wrows)
    win = pl.ds(y_pot, wrows)
    win_to = pl.ds(y_pot + 8, wrows)

    def own_orb(rows):
        return pltpu.make_async_copy(orb.at[0, :, pl.ds(y_mine, rows), :], orbs.at[t, inner, :rows, :], loc.at[0])

    def own_tri(rows):
        return pltpu.make_async_copy(tri.at[:, :, pl.ds(y_mine, rows), :], wide.at[z, :, inner, :rows, :], loc.at[1])

    locals_ = [
        pltpu.make_async_copy(ene, ene_m, loc.at[2]),
        pltpu.make_async_copy(che, che_m, loc.at[3]),
        pltpu.make_async_copy(shi, shi_m, loc.at[4]),
        pltpu.make_async_copy(pot.at[:, win, :], pots.at[2 : planes + 2, win_to, :], loc.at[5]),
        pltpu.make_async_copy(order, picks, loc.at[6]),
    ]
    def device(k):
        dt, ds, df = k // (ns * nf), (k // nf) % ns, k % nf
        return lax.rem(t + dt, nt), lax.rem(s + ds, ns), lax.rem(f + df, nf)

    count = nt * ns * nf
    barrier = pltpu.get_barrier_semaphore()
    below, above = jnp.maximum(s - 1, 0), jnp.minimum(s + 1, ns - 1)
    near_z = z + 1 - 2 * lax.rem(z, 2)
    if chips == 4:
        two, three = lax.rem(z + 2, chips), lax.rem(near_z + 2, chips)
        peers = [near_z, two, three]
        froms = [near_z, two, three]
    else:
        peers = [lax.rem(z + k, chips) for k in range(1, chips)]
        froms = [lax.rem(z + chips - k, chips) for k in range(1, chips)]

    def greet(**where):
        pl.semaphore_signal(barrier, inc=1, device_id=where, device_id_type=MESH)

    if near:
        for p in peers:
            greet(trial=2 * p + c)
        greet(trial=mate)
        for j in range(1, ns):
            greet(slab=lax.rem(s + j, ns))
        for j in range(1, nf):
            greet(freq=lax.rem(f + j, nf))
        greeted = chips + ns + nf - 2
    else:

        @pl.loop(1, count)
        def _(k):
            pt, ps, pf = device(k)
            greet(trial=pt, slab=ps, freq=pf)

        greeted = count - 1

    for copy in locals_[:3]:
        copy.start()
    sized(z, lambda rows: own_orb(rows).start())
    for copy in locals_[3:]:
        copy.start()
    sized(z, lambda rows: own_tri(rows).start())

    pots[:, 0:8, :] = jnp.zeros((planes + 4, 8, nz), jnp.float32)
    pots[:, ny + 8 :, :] = jnp.zeros((planes + 4, 8, nz), jnp.float32)

    @pl.when(last)
    def _():
        orbs[:, over] = jnp.zeros((norb, REACH) + orbs.shape[2:], jnp.float32)
        wide[:, :, over] = jnp.zeros((chips, per, REACH) + wide.shape[3:], jnp.float32)
        pots[planes + 2 :] = jnp.zeros((2,) + pots.shape[1:], jnp.float32)

    @pl.when(first)
    def _():
        orbs[:, under] = jnp.zeros((norb, UNDER) + orbs.shape[2:], jnp.float32)
        wide[:, :, under] = jnp.zeros((chips, per, UNDER) + wide.shape[3:], jnp.float32)
        pots[:2] = jnp.zeros((2,) + pots.shape[1:], jnp.float32)

    @pl.when(beyond(z))
    def _():
        orbs[:, :, mine:tall, :] = jnp.zeros((norb, deep, REACH, nz), jnp.float32)
        wide[:, :, :, mine:tall, :] = jnp.zeros((chips, per, deep, REACH, nz), jnp.float32)

    for copy in locals_[:3]:
        copy.wait()
    pars[t] = jnp.full((8, nz), ene_m[0], jnp.float32)
    row = lax.broadcasted_iota(jnp.int32, (8, nz), 0)
    tile = jnp.full((8, nz), shi_m[0], jnp.float32)
    for n in range(4):
        tile = jnp.where(row == n, che_m[0, n], tile)
    freqs[f] = tile
    sized(z, lambda rows: own_orb(rows).wait())

    pl.semaphore_wait(barrier, greeted)

    def remote(src, dst, send, recv, **where):
        return pltpu.make_async_remote_copy(
            src_ref=src, dst_ref=dst, send_sem=send, recv_sem=recv, device_id=where, device_id_type=MESH
        )

    def rows_at(p, rows):
        return pl.ds(f * half + p * mine, rows)

    def orb_out(p, rows):
        source = orb.at[0, :, rows_at(p, rows), :]
        return remote(source, orbs.at[t, inner, :rows, :], orb_s.at[p], orb_r.at[z, 0], trial=2 * p + c)

    def orb_in(p, rows):
        block = orbs.at[2 * p + c, inner, :rows, :]
        return remote(block, block, orb_s.at[p], orb_r.at[p, 0], trial=mate)

    def orb_mate(u, rows):
        block = orbs.at[u, inner, :rows, :]
        return remote(block, block, orb_s.at[chips], orb_x.at[0], trial=mate)

    def short(rows):
        return min(rows, mine + 2)

    def orb_halo(p, way, rows):
        u = 2 * p + c
        n = short(rows)
        if way == 0:
            source, there = orbs.at[u, planes : planes + UNDER, :n, :], orbs.at[u, under, :n, :]
            return remote(source, there, orb_s.at[chips + 1], orb_r.at[p, 1], slab=above)
        source, there = orbs.at[u, UNDER : UNDER + REACH, :n, :], orbs.at[u, over, :n, :]
        return remote(source, there, orb_s.at[chips + 2], orb_r.at[p, 2], slab=below)

    def halo_mate(u, way, rows):
        block = orbs.at[u, under if way == 0 else over, : short(rows), :]
        return remote(block, block, orb_s.at[chips + 3 + way], orb_x.at[1 + way], trial=mate)

    def par_out(p):
        return remote(pars.at[t], pars.at[t], par_s.at[0], par_r.at[z], trial=2 * p + c)

    def par_mate(p, u):
        return remote(pars.at[u], pars.at[u], par_s.at[0], par_x.at[0], trial=mate)

    def par_in(p):
        block = pars.at[2 * p + c]
        return remote(block, block, par_s.at[0], par_r.at[p], trial=mate)

    def shared(block, send, recv):
        return remote(block, block, send, recv, trial=mate)

    def pot_halo(way):
        if way == 0:
            source, there = pot.at[planes - 2 :, win, :], pots.at[:2, win_to, :]
            return remote(source, there, pot_s.at[0], pot_r.at[0], slab=above)
        source, there = pot.at[:2, win, :], pots.at[planes + 2 :, win_to, :]
        return remote(source, there, pot_s.at[1], pot_r.at[1], slab=below)

    def freq_copy(j):
        return remote(freqs.at[f], freqs.at[f], frq_s.at[j], frq_r.at[j], freq=lax.rem(f + j, nf))

    flip = first & (ns > 1)

    def start(h):
        return jnp.where(flip, sizes_[1], 0) if h == 0 else jnp.where(flip, 0, sizes_[0])

    def held(h):
        return pl.ds(UNDER + start(h), sizes_[h])

    def tri_out(p, h, rows):
        source = tri.at[:, pl.ds(start(h), sizes_[h]), rows_at(p, rows), :]
        there = wide.at[z, :, held(h), :rows, :]
        return remote(source, there, tri_s.at[p], tri_r.at[z, h], trial=2 * p + c)

    def tri_in(p, h, rows):
        block = wide.at[p, :, held(h), :rows, :]
        return remote(block, block, tri_s.at[p], tri_r.at[p, h], trial=mate)

    def tri_mate(p, h):
        source = wide.at[p, :, held(h), :mine, :]
        there = other.at[p, :, pl.ds(start(h), sizes_[h])]
        return remote(source, there, fwd_s.at[0], fwd_r.at[p, h], trial=mate)

    def tri_halo(p, way, rows):
        n = short(rows)
        if way == 0:
            source, there = wide.at[p, :, planes : planes + UNDER, :n, :], wide.at[p, :, under, :n, :]
            return remote(source, there, fwd_s.at[1], fwd_r.at[p, 2], slab=above)
        source, there = wide.at[p, :, UNDER : UNDER + REACH, :n, :], wide.at[p, :, over, :n, :]
        return remote(source, there, fwd_s.at[2], fwd_r.at[p, 3], slab=below)

    def orb_spread(p):
        u = 2 * p + c
        sized(z, lambda rows: when(down, lambda: orb_halo(p, 1, rows).start()))
        sized(z, lambda rows: when(up, lambda: orb_halo(p, 0, rows).start()))
        sized(z, lambda rows: orb_mate(u, rows).start())
        par_mate(p, u).start()

    def tri_spread(p, h):
        if h == 0:
            sized(z, lambda rows: when(down, lambda: tri_halo(p, 1, rows).start()))
            sized(z, lambda rows: when(up & flip, lambda: tri_halo(p, 0, rows).start()))
        else:
            sized(z, lambda rows: when(up & jnp.logical_not(flip), lambda: tri_halo(p, 0, rows).start()))
        tri_mate(p, h).start()

    for p in peers:
        sized(p, lambda rows: orb_out(p, rows).start())
        par_out(p).start()
    orb_spread(z)
    for j in range(1, nf):
        freq_copy(j).start()
    when(up, lambda: pot_halo(0).start())
    when(down, lambda: pot_halo(1).start())
    for n, h in [(0, 0), (0, 1)] + [(n, h) for h in range(PIECES) for n in range(1, chips - 1)]:
        sized(peers[n], lambda rows: tri_out(peers[n], h, rows).start())

    for p in froms:
        sized(z, lambda rows: orb_in(p, rows).wait_recv())
        par_in(p).wait_recv()
        orb_spread(p)
    sized(z, lambda rows: own_tri(rows).wait())
    for h in range(PIECES):
        tri_spread(z, h)
    for p in [z] + froms:

        def pass_on(rows):
            def side(way):
                orb_halo(p, way, rows).wait_recv()
                halo_mate(2 * p + c, way, rows).start()

            when(up, lambda: side(1))
            when(down, lambda: side(0))

        sized(z, pass_on)

    for copy in locals_[3:]:
        copy.wait()
    for j in range(1, nf):
        freq_copy(j).wait_recv()
    some = slice(0, chips)

    def waits(rows):
        n = short(rows)
        shared(orbs.at[some, inner, :rows, :], orb_s.at[chips], orb_x.at[0]).wait_recv()
        when(down, lambda: shared(orbs.at[some, under, :n, :], orb_s.at[chips], orb_x.at[1]).wait_recv())
        when(up, lambda: shared(orbs.at[some, over, :n, :], orb_s.at[chips], orb_x.at[2]).wait_recv())

    sized(z, waits)
    shared(pars.at[some], par_s.at[0], par_x.at[0]).wait_recv()
    if near:
        for j in range(1, nf):
            pl.semaphore_signal(gate, inc=1, device_id={"freq": lax.rem(f + j, nf)}, device_id_type=MESH)
    when(up, lambda: pot_halo(1).wait_recv())
    when(down, lambda: pot_halo(0).wait_recv())

    inverse = 1.0 / 4.5
    hop = -0.5 / 4.5

    for i in range(norb):
        energy = pars[i]
        terms = [0.0, 0.0, 0.0, 0.0]
        for w in range(nf):
            mu = (energy + freqs[w, 4:5, :]) * inverse
            c0, c1, c2, c3 = (freqs[w, n : 1 + n, :] for n in range(4))
            b0, b1, b2, b3 = c0 - c2, c1 - 3.0 * c3, 2.0 * c2, 4.0 * c3
            terms[0] += b0 - mu * (b1 - mu * (b2 - mu * b3))
            terms[1] += b1 - mu * (2.0 * b2 - 3.0 * mu * b3)
            terms[2] += b2 - 3.0 * mu * b3
            terms[3] += b3
        for n in range(4):
            weights[n, i] = jnp.broadcast_to(terms[n], (8, nz))

    lane = lax.broadcasted_iota(jnp.int32, (mine, nz), 1)
    rows_ = lax.broadcasted_iota(jnp.int32, (mine, nz), 0) + y_mine

    def links(position, size):
        return (position >= 1).astype(jnp.float32) + (position + 1 < size).astype(jnp.float32)

    def coef_plane(x, carry):
        column = jnp.zeros((mine, nz), jnp.int32) + (s * planes + x)
        for dz in range(-REACH, REACH + 1):
            group = [(n, off) for n, off in enumerate(OFFSETS) if off[2] == dz]
            if not group:
                continue
            depth = lane - dz
            inside = ((depth >= 0) & (depth < nz)).astype(jnp.float32)
            least = min(sum(map(abs, off)) for _, off in group)
            scaled = {}
            for i in range(norb):
                centre = rolled(orbs[i, UNDER + x, :mine, :], dz) * inside
                for n in range(least, 4):
                    scaled[n, i] = weights[n, i, :mine, :] * centre

            def local(a, b, e):
                return rolled(pots[2 + x + a, pl.ds(8 + y_mine + b, mine), :], dz - e) * inverse

            for index, (dx, dy, _) in group:
                steps = abs(dx) + abs(dy) + abs(dz)
                sums = {n: 0.0 for n in range(steps, 4)}
                for i in range(norb):
                    there = orbs[i, UNDER + x + dx, dy : dy + mine, :]
                    for n in sums:
                        sums[n] = sums[n] + scaled[n, i] * there
                if steps == 3:
                    kind = tuple(sorted(map(abs, (dx, dy, dz))))
                    coef = (PATHS[kind] * hop**3) * sums[3]
                elif steps == 2:
                    here, end = local(0, 0, 0), local(dx, dy, dz)
                    corners = [p for p in ((dx, 0, 0), (0, dy, 0), (0, 0, dz)) if p != (0, 0, 0)]
                    if len(corners) == 1:
                        middle = local(int(dx / 2), int(dy / 2), int(dz / 2))
                        coef = hop**2 * (sums[2] + (here + middle + end) * sums[3])
                    else:
                        middle = local(*corners[0]) + local(*corners[1])
                        coef = hop**2 * (2.0 * sums[2] + (2.0 * (here + end) + middle) * sums[3])
                elif steps == 1:
                    here, end = local(0, 0, 0), local(dx, dy, dz)
                    place = (column, rows_, depth)
                    size = (planes * ns, ny, nz)
                    move = (dx, dy, dz)
                    side, along = 0.0, 0.0
                    for axis in range(3):
                        if move[axis]:
                            along = links(place[axis], size[axis]) + links(place[axis] + move[axis], size[axis])
                        else:
                            side = side + links(place[axis], size[axis])
                    walks = along + 3.0 * side - 1.0
                    cubic = here * here + here * end + end * end + hop**2 * walks
                    coef = hop * (sums[1] + (here + end) * sums[2] + cubic * sums[3])
                else:
                    here = local(0, 0, 0)
                    degree = links(column, planes * ns) + links(rows_, ny) + links(lane, nz)
                    beside = local(1, 0, 0) + local(-1, 0, 0) + local(0, 1, 0) + local(0, -1, 0)
                    beside = beside + jnp.where(lane + 1 < nz, local(0, 0, 1), 0.0)
                    beside = beside + jnp.where(lane >= 1, local(0, 0, -1), 0.0)
                    square = here * here + hop**2 * degree
                    cube = here * (here * here + 2.0 * hop**2 * degree) + hop**2 * beside
                    coef = 0.5 * (sums[0] + here * sums[1] + square * sums[2] + cube * sums[3])
                coefs[x, index] = coef
        return carry

    lax.fori_loop(0, planes, coef_plane, 0)

    def density(p):
        def halos(rows):
            when(up, lambda: tri_halo(p, 1, rows).wait_recv())
            when(down, lambda: tri_halo(p, 0, rows).wait_recv())

        sized(z, halos)

        def plane_step(x, carry):
            sums_ = [0.0] * per
            for dz in range(-REACH, REACH + 1):
                group = [(n, off) for n, off in enumerate(OFFSETS) if off[2] == dz]
                if not group:
                    continue
                sums = [0.0] * per
                for index, (dx, dy, _) in group:
                    coef = coefs[x, index]
                    for k in range(per):
                        sums[k] = sums[k] + coef * wide[p, k, UNDER + x + dx, dy : dy + mine, :]
                for k in range(per):
                    sums_[k] = sums_[k] + rolled(sums[k], -dz)
            for k in range(per):
                dens[p, k, x] = sums_[k]
            return carry

        lax.fori_loop(0, planes, plane_step, 0)

    def take(n, h):
        p = froms[n]
        sized(z, lambda rows: tri_in(p, h, rows).wait_recv())
        tri_spread(p, h)

    contract = (((1,), (1,)), ((), ()))

    work = [z] + froms
    both = 2 * per

    def ready(n, h):
        p = work[n]
        tri_mate(p, h).wait_recv()
        for k in range(sizes_[h]):
            x = start(h) + k
            for r in range(mine):
                value = jnp.concatenate([wide[p, :, UNDER + x, r, :], other[p, :, x, r, :]], axis=0)
                high = value.astype(jnp.bfloat16)
                cut = slice(r * nz, (r + 1) * nz)
                t_high[x, n * both : (n + 1) * both, cut] = high
                t_low[x, n * both : (n + 1) * both, cut] = (value - high.astype(jnp.float32)).astype(jnp.bfloat16)

    def weighed(n):
        p = work[n]

        def plane_step(x, carry):
            for r in range(mine):
                value = dens[p, :, x, r, :]
                high = value.astype(jnp.bfloat16).astype(jnp.float32)
                pair = jnp.concatenate([high, value - high], axis=0)
                d_both[x, n * both : (n + 1) * both, r * nz : (r + 1) * nz] = pair.astype(jnp.bfloat16)
            return carry

        lax.fori_loop(0, planes, plane_step, 0)

    def dots(h, lo, hi):
        acc = jnp.zeros((chips * both, (hi - lo) * both), jnp.float32)
        for k in range(sizes_[h]):
            x = start(h) + k
            right = d_both[x, lo * both : hi * both, :]
            for left in (t_high, t_low):
                acc = acc + lax.dot_general(left[x], right, contract, preferred_element_type=jnp.float32)
        return acc

    for h in range(PIECES):
        take(0, h)
    density(work[0])
    for h in range(PIECES):
        ready(0, h)
    weighed(0)
    take(1, 0)
    density(work[1])
    for h in range(PIECES):
        ready(1, h)
    weighed(1)
    for n in range(2, chips - 1):
        take(n, 0)
    for n in range(2, chips):
        ready(n, 0)
    early = dots(0, 0, 2)
    for n in range(1, chips - 1):
        take(n, 1)
        density(work[n + 1])
        weighed(n + 1)
    for n in range(2, chips):
        ready(n, 1)
    early = early + dots(1, 0, 2)
    late = sum(dots(h, 2, chips) for h in range(PIECES))
    gram = jnp.concatenate([early, late], axis=1)
    index = lax.broadcasted_iota(jnp.int32, (total, total), 0)
    chip = jnp.zeros((total, total), jnp.int32)
    for n, p in enumerate(work):
        chip = jnp.where(index // both == n, p, chip)
    inside = lax.rem(index, per)
    far_core = lax.rem(index // per, 2)
    pick = (picks[...] == (2 * chip + c + far_core * (1 - 2 * c)) * per + inside).astype(jnp.float32)
    chosen = (picks[...] == (2 * chip + c) * per + inside).astype(jnp.float32)
    factor = 1.0 / jnp.sqrt(jnp.float32(planes * ns * ny * nz * norb))
    moved = lax.dot_general(
        pick, gram * factor, (((0,), (0,)), ((), ())), precision=lax.Precision.HIGH, preferred_element_type=jnp.float32
    )
    final = jnp.dot(moved, chosen, precision=lax.Precision.HIGH, preferred_element_type=jnp.float32)
    final = final + final.T
    owned = total // (nt * ns)
    for r in range(nt * ns):
        rows_out[r] = final[r * owned : (r + 1) * owned]
    if near:
        for j in range(1, nf):
            pl.semaphore_wait(gate, 1)

    def me():
        return (t * ns + s) * nf + f

    def row_copy(k):
        pt, ps, pf = device(k)
        return remote(
            rows_out.at[pt * ns + ps], rows_in.at[me()], row_s.at[0], row_r.at[0], trial=pt, slab=ps, freq=pf
        )

    def each(action):
        if count <= 64:
            for k in range(1, count):
                action(k)
        else:
            pl.loop(1, count)(action)

    each(lambda k: row_copy(k).start())
    rows_in[me()] = rows_out[t * ns + s]
    for j in range(1, nf):
        freq_copy(j).wait_send()
    when(up, lambda: pot_halo(0).wait_send())
    when(down, lambda: pot_halo(1).wait_send())
    for p in peers:

        def out_waits(rows):
            orb_out(p, rows).wait_send()
            shared(wide.at[p, :, inner, :rows, :], tri_s.at[p], tri_r.at[p, 0]).wait_send()

        sized(p, out_waits)
    shared(pars.at[: nt - 1], par_s.at[0], par_x.at[0]).wait_send()
    shared(other, fwd_s.at[0], fwd_r.at[0, 0]).wait_send()

    def sends(rows):
        n = short(rows)
        shared(orbs.at[some, inner, :rows, :], orb_s.at[chips], orb_x.at[0]).wait_send()

        @pl.when(up)
        def _():
            shared(orbs.at[some, under, :n, :], orb_s.at[chips + 1], orb_x.at[0]).wait_send()
            shared(orbs.at[some, over, :n, :], orb_s.at[chips + 4], orb_x.at[0]).wait_send()
            shared(wide.at[:, :, under, :n, :], fwd_s.at[1], orb_x.at[0]).wait_send()

        @pl.when(down)
        def _():
            shared(orbs.at[some, over, :n, :], orb_s.at[chips + 2], orb_x.at[0]).wait_send()
            shared(orbs.at[some, under, :n, :], orb_s.at[chips + 3], orb_x.at[0]).wait_send()
            shared(wide.at[:, :, over, :n, :], fwd_s.at[2], orb_x.at[0]).wait_send()

    sized(z, sends)
    rest = rows_in.at[: count - 1]
    remote(rest, rest, row_s.at[0], row_r.at[0], trial=mate).wait()
    out[...] = jnp.sum(rows_in[...], axis=0)


def local(sizes, orbitals, energies, potential, trials, cheb, shifts, column_order):
    nt, ns, nf = sizes
    per, planes, ny, nz = trials.shape
    norb = orbitals.shape[0] * nt
    chips = nt // 2
    mine = ny // nf // chips
    tall = -(-(mine + REACH) // 8) * 8
    deep = planes + UNDER + REACH
    total = nt * per
    owned = total // (nt * ns)
    count = nt * ns * nf
    f32 = jnp.float32
    dma = pltpu.SemaphoreType.DMA
    anywhere = pl.BlockSpec(memory_space=pltpu.HBM)
    return pl.pallas_call(
        functools.partial(kernel, sizes),
        out_shape=jax.ShapeDtypeStruct((owned, total), f32),
        in_specs=[anywhere] * 7,
        out_specs=pl.BlockSpec(memory_space=pltpu.VMEM),
        scratch_shapes=[
            pltpu.VMEM((norb, deep, tall, nz), f32),
            pltpu.VMEM((chips, per, deep, tall, nz), f32),
            pltpu.VMEM((chips, per, planes, mine, nz), f32),
            pltpu.VMEM((planes + 4, ny + 16, nz), f32),
            pltpu.VMEM((norb, 8, nz), f32),
            pltpu.VMEM((nf, 8, nz), f32),
            pltpu.VMEM((4, norb, 8, nz), f32),
            pltpu.VMEM((planes, len(OFFSETS), mine, nz), f32),
            pltpu.VMEM((chips, per, planes, mine, nz), f32),
            pltpu.VMEM((planes, total, mine * nz), jnp.bfloat16),
            pltpu.VMEM((planes, total, mine * nz), jnp.bfloat16),
            pltpu.VMEM((planes, total, mine * nz), jnp.bfloat16),
            pltpu.VMEM((nt * ns, owned, total), f32),
            pltpu.VMEM((count, owned, total), f32),
            pltpu.SMEM((1,), f32),
            pltpu.SMEM((1, 4), f32),
            pltpu.SMEM((1,), f32),
            pltpu.VMEM((1, total), jnp.int32),
            dma((chips + 5,)), dma((chips, 3)), dma((3,)), dma((1,)), dma((chips,)), dma((1,)),
            dma((2,)), dma((2,)), dma((nf,)), dma((nf,)),
            dma((chips,)), dma((chips, PIECES)), dma((3,)), dma((chips, 4)),
            dma((1,)), dma((1,)),
            dma((7,)),
            pltpu.SemaphoreType.REGULAR,
        ],
        compiler_params=pltpu.CompilerParams(
            collective_id=0, has_side_effects=True, vmem_limit_bytes=67043328 - 65536
        ),
    )(orbitals, energies, potential, trials, cheb, shifts, column_order[None])


def solution(mesh):
    sizes = tuple(mesh.shape[name] for name in ("trial", "slab", "freq"))
    in_specs = (
        P("trial", "slab", None, None),
        P("trial"),
        P("slab", None, None),
        P("trial", "slab", None, None),
        P("freq", None),
        P("freq"),
        P(),
    )
    out_specs = P(("trial", "slab"), None)
    return jax.shard_map(
        functools.partial(local, sizes), mesh=mesh, in_specs=in_specs, out_specs=out_specs, check_vma=False
    )
```

```python
import functools

import jax
import jax.numpy as jnp
from jax import lax
from jax.experimental import pallas as pl
from jax.experimental.pallas import tpu as pltpu
from jax.sharding import PartitionSpec as P

REACH = 3
UNDER = 2
MESH = pl.DeviceIdType.MESH

OFFSETS = [
    (dx, dy, dz)
    for dz in range(-REACH, REACH + 1)
    for dx in range(-REACH, REACH + 1)
    for dy in range(REACH + 1)
    if abs(dx) + abs(dy) + abs(dz) <= REACH and (dy, dx, dz) >= (0, 0, 0)
]
PATHS = {(1, 1, 1): 6.0, (0, 1, 2): 3.0, (0, 0, 3): 1.0}
PIECES = 2


def rolled(value, shift):
    shift = shift % value.shape[1]
    return value if shift == 0 else pltpu.roll(value, shift, 1)


def when(condition, action):
    pl.when(condition)(action)


def kernel(
    sizes, orb, ene, pot, tri, che, shi, order, out,
    orbs, wide, other, pots, pars, freqs, weights, coefs, dens, t_high, t_low, d_both, rows_out, rows_in,
    ene_m, che_m, shi_m, picks,
    orb_s, orb_r, orb_x, par_s, par_r, par_x, pot_s, pot_r, frq_s, frq_r,
    tri_s, tri_r, fwd_s, fwd_r, row_s, row_r, loc, gate,
):
    nt, ns, nf = sizes
    per, planes, ny, nz = tri.shape
    norb = orbs.shape[0]
    half = ny // nf
    total = nt * per
    chips = nt // 2
    mine = half // chips
    tall = mine + REACH
    sizes_ = (min(REACH, planes - 1), planes - min(REACH, planes - 1))
    deep = planes + UNDER + REACH
    t, s, f = lax.axis_index("trial"), lax.axis_index("slab"), lax.axis_index("freq")
    z, c = t // 2, lax.rem(t, 2)
    mate = t + 1 - 2 * c
    first, last = s == 0, s == ns - 1
    up, down = s < ns - 1, s > 0
    inner = slice(UNDER, UNDER + planes)
    over, under = slice(UNDER + planes, deep), slice(0, UNDER)
    near = ns <= 2 and nf <= 2
    y_mine = f * half + z * mine

    def beyond(zz):
        return (f == nf - 1) & (zz == chips - 1)

    def sized(zz, action):
        when(beyond(zz), lambda: action(mine))
        when(jnp.logical_not(beyond(zz)), lambda: action(tall))

    wrows = min(mine + 16, ny)
    y_pot = jnp.clip(y_mine - 8, 0, ny - wrows)
    win = pl.ds(y_pot, wrows)
    win_to = pl.ds(y_pot + 8, wrows)

    def own_orb(rows):
        return pltpu.make_async_copy(orb.at[0, :, pl.ds(y_mine, rows), :], orbs.at[t, inner, :rows, :], loc.at[0])

    def own_tri(rows):
        return pltpu.make_async_copy(tri.at[:, :, pl.ds(y_mine, rows), :], wide.at[z, :, inner, :rows, :], loc.at[1])

    locals_ = [
        pltpu.make_async_copy(ene, ene_m, loc.at[2]),
        pltpu.make_async_copy(che, che_m, loc.at[3]),
        pltpu.make_async_copy(shi, shi_m, loc.at[4]),
        pltpu.make_async_copy(pot.at[:, win, :], pots.at[2 : planes + 2, win_to, :], loc.at[5]),
        pltpu.make_async_copy(order, picks, loc.at[6]),
    ]
    def device(k):
        dt, ds, df = k // (ns * nf), (k // nf) % ns, k % nf
        return lax.rem(t + dt, nt), lax.rem(s + ds, ns), lax.rem(f + df, nf)

    count = nt * ns * nf
    barrier = pltpu.get_barrier_semaphore()
    below, above = jnp.maximum(s - 1, 0), jnp.minimum(s + 1, ns - 1)
    near_z = z + 1 - 2 * lax.rem(z, 2)
    if chips == 4:
        two, three = lax.rem(z + 2, chips), lax.rem(near_z + 2, chips)
        peers = [near_z, two, three]
        froms = [near_z, two, three]
    else:
        peers = [lax.rem(z + k, chips) for k in range(1, chips)]
        froms = [lax.rem(z + chips - k, chips) for k in range(1, chips)]

    def greet(**where):
        pl.semaphore_signal(barrier, inc=1, device_id=where, device_id_type=MESH)

    if near:
        for p in peers:
            greet(trial=2 * p + c)
        greet(trial=mate)
        for j in range(1, ns):
            greet(slab=lax.rem(s + j, ns))
        for j in range(1, nf):
            greet(freq=lax.rem(f + j, nf))
        greeted = chips + ns + nf - 2
    else:

        @pl.loop(1, count)
        def _(k):
            pt, ps, pf = device(k)
            greet(trial=pt, slab=ps, freq=pf)

        greeted = count - 1

    for copy in locals_[:3]:
        copy.start()
    sized(z, lambda rows: own_orb(rows).start())
    for copy in locals_[3:]:
        copy.start()
    sized(z, lambda rows: own_tri(rows).start())

    pots[:, 0:8, :] = jnp.zeros((planes + 4, 8, nz), jnp.float32)
    pots[:, ny + 8 :, :] = jnp.zeros((planes + 4, 8, nz), jnp.float32)

    @pl.when(last)
    def _():
        orbs[:, over] = jnp.zeros((norb, REACH) + orbs.shape[2:], jnp.float32)
        wide[:, :, over] = jnp.zeros((chips, per, REACH) + wide.shape[3:], jnp.float32)
        pots[planes + 2 :] = jnp.zeros((2,) + pots.shape[1:], jnp.float32)

    @pl.when(first)
    def _():
        orbs[:, under] = jnp.zeros((norb, UNDER) + orbs.shape[2:], jnp.float32)
        wide[:, :, under] = jnp.zeros((chips, per, UNDER) + wide.shape[3:], jnp.float32)
        pots[:2] = jnp.zeros((2,) + pots.shape[1:], jnp.float32)

    @pl.when(beyond(z))
    def _():
        orbs[:, :, mine:tall, :] = jnp.zeros((norb, deep, REACH, nz), jnp.float32)
        wide[:, :, :, mine:tall, :] = jnp.zeros((chips, per, deep, REACH, nz), jnp.float32)

    for copy in locals_[:3]:
        copy.wait()
    pars[t] = jnp.full((8, nz), ene_m[0], jnp.float32)
    row = lax.broadcasted_iota(jnp.int32, (8, nz), 0)
    tile = jnp.full((8, nz), shi_m[0], jnp.float32)
    for n in range(4):
        tile = jnp.where(row == n, che_m[0, n], tile)
    freqs[f] = tile
    sized(z, lambda rows: own_orb(rows).wait())

    pl.semaphore_wait(barrier, greeted)

    def remote(src, dst, send, recv, **where):
        return pltpu.make_async_remote_copy(
            src_ref=src, dst_ref=dst, send_sem=send, recv_sem=recv, device_id=where, device_id_type=MESH
        )

    def rows_at(p, rows):
        return pl.ds(f * half + p * mine, rows)

    def orb_out(p, rows):
        source = orb.at[0, :, rows_at(p, rows), :]
        return remote(source, orbs.at[t, inner, :rows, :], orb_s.at[p], orb_r.at[z, 0], trial=2 * p + c)

    def orb_in(p, rows):
        block = orbs.at[2 * p + c, inner, :rows, :]
        return remote(block, block, orb_s.at[p], orb_r.at[p, 0], trial=mate)

    def orb_mate(u, rows):
        block = orbs.at[u, inner, :rows, :]
        return remote(block, block, orb_s.at[chips], orb_x.at[0], trial=mate)

    def short(rows):
        return min(rows, mine + 2)

    def orb_halo(p, way, rows):
        u = 2 * p + c
        n = short(rows)
        if way == 0:
            source, there = orbs.at[u, planes : planes + UNDER, :n, :], orbs.at[u, under, :n, :]
            return remote(source, there, orb_s.at[chips + 1], orb_r.at[p, 1], slab=above)
        source, there = orbs.at[u, UNDER : UNDER + REACH, :n, :], orbs.at[u, over, :n, :]
        return remote(source, there, orb_s.at[chips + 2], orb_r.at[p, 2], slab=below)

    def halo_mate(u, way, rows):
        block = orbs.at[u, under if way == 0 else over, : short(rows), :]
        return remote(block, block, orb_s.at[chips + 3 + way], orb_x.at[1 + way], trial=mate)

    def par_out(p):
        return remote(pars.at[t], pars.at[t], par_s.at[0], par_r.at[z], trial=2 * p + c)

    def par_mate(p, u):
        return remote(pars.at[u], pars.at[u], par_s.at[0], par_x.at[0], trial=mate)

    def par_in(p):
        block = pars.at[2 * p + c]
        return remote(block, block, par_s.at[0], par_r.at[p], trial=mate)

    def shared(block, send, recv):
        return remote(block, block, send, recv, trial=mate)

    def pot_halo(way):
        if way == 0:
            source, there = pot.at[planes - 2 :, win, :], pots.at[:2, win_to, :]
            return remote(source, there, pot_s.at[0], pot_r.at[0], slab=above)
        source, there = pot.at[:2, win, :], pots.at[planes + 2 :, win_to, :]
        return remote(source, there, pot_s.at[1], pot_r.at[1], slab=below)

    def freq_copy(j):
        return remote(freqs.at[f], freqs.at[f], frq_s.at[j], frq_r.at[j], freq=lax.rem(f + j, nf))

    flip = first & (ns > 1)

    def start(h):
        return jnp.where(flip, sizes_[1], 0) if h == 0 else jnp.where(flip, 0, sizes_[0])

    def held(h):
        return pl.ds(UNDER + start(h), sizes_[h])

    def tri_out(p, h, rows):
        source = tri.at[:, pl.ds(start(h), sizes_[h]), rows_at(p, rows), :]
        there = wide.at[z, :, held(h), :rows, :]
        return remote(source, there, tri_s.at[p], tri_r.at[z, h], trial=2 * p + c)

    def tri_in(p, h, rows):
        block = wide.at[p, :, held(h), :rows, :]
        return remote(block, block, tri_s.at[p], tri_r.at[p, h], trial=mate)

    def tri_mate(p, h):
        source = wide.at[p, :, held(h), :mine, :]
        there = other.at[p, :, pl.ds(start(h), sizes_[h])]
        return remote(source, there, fwd_s.at[0], fwd_r.at[p, h], trial=mate)

    def tri_halo(p, way, rows):
        n = short(rows)
        if way == 0:
            source, there = wide.at[p, :, planes : planes + UNDER, :n, :], wide.at[p, :, under, :n, :]
            return remote(source, there, fwd_s.at[1], fwd_r.at[p, 2], slab=above)
        source, there = wide.at[p, :, UNDER : UNDER + REACH, :n, :], wide.at[p, :, over, :n, :]
        return remote(source, there, fwd_s.at[2], fwd_r.at[p, 3], slab=below)

    def orb_spread(p):
        u = 2 * p + c
        sized(z, lambda rows: when(down, lambda: orb_halo(p, 1, rows).start()))
        sized(z, lambda rows: when(up, lambda: orb_halo(p, 0, rows).start()))
        sized(z, lambda rows: orb_mate(u, rows).start())
        par_mate(p, u).start()

    def tri_spread(p, h):
        if h == 0:
            sized(z, lambda rows: when(down, lambda: tri_halo(p, 1, rows).start()))
            sized(z, lambda rows: when(up & flip, lambda: tri_halo(p, 0, rows).start()))
        else:
            sized(z, lambda rows: when(up & jnp.logical_not(flip), lambda: tri_halo(p, 0, rows).start()))
        tri_mate(p, h).start()

    for p in peers:
        sized(p, lambda rows: orb_out(p, rows).start())
        par_out(p).start()
    orb_spread(z)
    for j in range(1, nf):
        freq_copy(j).start()
    when(up, lambda: pot_halo(0).start())
    when(down, lambda: pot_halo(1).start())
    for n, h in [(0, 0), (0, 1)] + [(n, h) for h in range(PIECES) for n in range(1, chips - 1)]:
        sized(peers[n], lambda rows: tri_out(peers[n], h, rows).start())

    for p in froms:
        sized(z, lambda rows: orb_in(p, rows).wait_recv())
        par_in(p).wait_recv()
        orb_spread(p)
    sized(z, lambda rows: own_tri(rows).wait())
    for h in range(PIECES):
        tri_spread(z, h)
    for p in [z] + froms:

        def pass_on(rows):
            def side(way):
                orb_halo(p, way, rows).wait_recv()
                halo_mate(2 * p + c, way, rows).start()

            when(up, lambda: side(1))
            when(down, lambda: side(0))

        sized(z, pass_on)

    for copy in locals_[3:]:
        copy.wait()
    for j in range(1, nf):
        freq_copy(j).wait_recv()
    some = slice(0, chips)

    def waits(rows):
        n = short(rows)
        shared(orbs.at[some, inner, :rows, :], orb_s.at[chips], orb_x.at[0]).wait_recv()
        when(down, lambda: shared(orbs.at[some, under, :n, :], orb_s.at[chips], orb_x.at[1]).wait_recv())
        when(up, lambda: shared(orbs.at[some, over, :n, :], orb_s.at[chips], orb_x.at[2]).wait_recv())

    sized(z, waits)
    shared(pars.at[some], par_s.at[0], par_x.at[0]).wait_recv()
    if near:
        for j in range(1, nf):
            pl.semaphore_signal(gate, inc=1, device_id={"freq": lax.rem(f + j, nf)}, device_id_type=MESH)
    when(up, lambda: pot_halo(1).wait_recv())
    when(down, lambda: pot_halo(0).wait_recv())

    inverse = 1.0 / 4.5
    hop = -0.5 / 4.5

    for i in range(norb):
        energy = pars[i]
        terms = [0.0, 0.0, 0.0, 0.0]
        for w in range(nf):
            mu = (energy + freqs[w, 4:5, :]) * inverse
            c0, c1, c2, c3 = (freqs[w, n : 1 + n, :] for n in range(4))
            b0, b1, b2, b3 = c0 - c2, c1 - 3.0 * c3, 2.0 * c2, 4.0 * c3
            terms[0] += b0 - mu * (b1 - mu * (b2 - mu * b3))
            terms[1] += b1 - mu * (2.0 * b2 - 3.0 * mu * b3)
            terms[2] += b2 - 3.0 * mu * b3
            terms[3] += b3
        for n in range(4):
            weights[n, i] = jnp.broadcast_to(terms[n], (8, nz))

    lane = lax.broadcasted_iota(jnp.int32, (mine, nz), 1)
    rows_ = lax.broadcasted_iota(jnp.int32, (mine, nz), 0) + y_mine

    def links(position, size):
        return (position >= 1).astype(jnp.float32) + (position + 1 < size).astype(jnp.float32)

    def coef_plane(x, carry):
        column = jnp.zeros((mine, nz), jnp.int32) + (s * planes + x)
        for dz in range(-REACH, REACH + 1):
            group = [(n, off) for n, off in enumerate(OFFSETS) if off[2] == dz]
            if not group:
                continue
            depth = lane - dz
            inside = ((depth >= 0) & (depth < nz)).astype(jnp.float32)
            least = min(sum(map(abs, off)) for _, off in group)
            scaled = {}
            for i in range(norb):
                centre = rolled(orbs[i, UNDER + x, :mine, :], dz) * inside
                for n in range(least, 4):
                    scaled[n, i] = weights[n, i, :mine, :] * centre

            def local(a, b, e):
                return rolled(pots[2 + x + a, pl.ds(8 + y_mine + b, mine), :], dz - e) * inverse

            for index, (dx, dy, _) in group:
                steps = abs(dx) + abs(dy) + abs(dz)
                sums = {n: 0.0 for n in range(steps, 4)}
                for i in range(norb):
                    there = orbs[i, UNDER + x + dx, dy : dy + mine, :]
                    for n in sums:
                        sums[n] = sums[n] + scaled[n, i] * there
                if steps == 3:
                    kind = tuple(sorted(map(abs, (dx, dy, dz))))
                    coef = (PATHS[kind] * hop**3) * sums[3]
                elif steps == 2:
                    here, end = local(0, 0, 0), local(dx, dy, dz)
                    corners = [p for p in ((dx, 0, 0), (0, dy, 0), (0, 0, dz)) if p != (0, 0, 0)]
                    if len(corners) == 1:
                        middle = local(int(dx / 2), int(dy / 2), int(dz / 2))
                        coef = hop**2 * (sums[2] + (here + middle + end) * sums[3])
                    else:
                        middle = local(*corners[0]) + local(*corners[1])
                        coef = hop**2 * (2.0 * sums[2] + (2.0 * (here + end) + middle) * sums[3])
                elif steps == 1:
                    here, end = local(0, 0, 0), local(dx, dy, dz)
                    place = (column, rows_, depth)
                    size = (planes * ns, ny, nz)
                    move = (dx, dy, dz)
                    side, along = 0.0, 0.0
                    for axis in range(3):
                        if move[axis]:
                            along = links(place[axis], size[axis]) + links(place[axis] + move[axis], size[axis])
                        else:
                            side = side + links(place[axis], size[axis])
                    walks = along + 3.0 * side - 1.0
                    cubic = here * here + here * end + end * end + hop**2 * walks
                    coef = hop * (sums[1] + (here + end) * sums[2] + cubic * sums[3])
                else:
                    here = local(0, 0, 0)
                    degree = links(column, planes * ns) + links(rows_, ny) + links(lane, nz)
                    beside = local(1, 0, 0) + local(-1, 0, 0) + local(0, 1, 0) + local(0, -1, 0)
                    beside = beside + jnp.where(lane + 1 < nz, local(0, 0, 1), 0.0)
                    beside = beside + jnp.where(lane >= 1, local(0, 0, -1), 0.0)
                    square = here * here + hop**2 * degree
                    cube = here * (here * here + 2.0 * hop**2 * degree) + hop**2 * beside
                    coef = 0.5 * (sums[0] + here * sums[1] + square * sums[2] + cube * sums[3])
                coefs[x, index] = coef
        return carry

    lax.fori_loop(0, planes, coef_plane, 0)

    def density(p):
        def halos(rows):
            when(up, lambda: tri_halo(p, 1, rows).wait_recv())
            when(down, lambda: tri_halo(p, 0, rows).wait_recv())

        sized(z, halos)

        def plane_step(x, carry):
            sums_ = [0.0] * per
            for dz in range(-REACH, REACH + 1):
                group = [(n, off) for n, off in enumerate(OFFSETS) if off[2] == dz]
                if not group:
                    continue
                sums = [0.0] * per
                for index, (dx, dy, _) in group:
                    coef = coefs[x, index]
                    for k in range(per):
                        sums[k] = sums[k] + coef * wide[p, k, UNDER + x + dx, dy : dy + mine, :]
                for k in range(per):
                    sums_[k] = sums_[k] + rolled(sums[k], -dz)
            for k in range(per):
                dens[p, k, x] = sums_[k]
            return carry

        lax.fori_loop(0, planes, plane_step, 0)

    def take(n, h):
        p = froms[n]
        sized(z, lambda rows: tri_in(p, h, rows).wait_recv())
        tri_spread(p, h)

    contract = (((1,), (1,)), ((), ()))

    work = [z] + froms
    both = 2 * per

    def ready(n, h):
        p = work[n]
        tri_mate(p, h).wait_recv()
        for k in range(sizes_[h]):
            x = start(h) + k
            for r in range(mine):
                value = jnp.concatenate([wide[p, :, UNDER + x, r, :], other[p, :, x, r, :]], axis=0)
                high = value.astype(jnp.bfloat16)
                cut = slice(r * nz, (r + 1) * nz)
                t_high[x, n * both : (n + 1) * both, cut] = high
                t_low[x, n * both : (n + 1) * both, cut] = (value - high.astype(jnp.float32)).astype(jnp.bfloat16)

    def weighed(n):
        p = work[n]

        def plane_step(x, carry):
            for r in range(mine):
                value = dens[p, :, x, r, :]
                high = value.astype(jnp.bfloat16).astype(jnp.float32)
                pair = jnp.concatenate([high, value - high], axis=0)
                d_both[x, n * both : (n + 1) * both, r * nz : (r + 1) * nz] = pair.astype(jnp.bfloat16)
            return carry

        lax.fori_loop(0, planes, plane_step, 0)

    def dots(h, lo, hi):
        acc = jnp.zeros((chips * both, (hi - lo) * both), jnp.float32)
        for k in range(sizes_[h]):
            x = start(h) + k
            right = d_both[x, lo * both : hi * both, :]
            for left in (t_high, t_low):
                acc = acc + lax.dot_general(left[x], right, contract, preferred_element_type=jnp.float32)
        return acc

    for h in range(PIECES):
        take(0, h)
    density(work[0])
    for h in range(PIECES):
        ready(0, h)
    weighed(0)
    take(1, 0)
    density(work[1])
    for h in range(PIECES):
        ready(1, h)
    weighed(1)
    for n in range(2, chips - 1):
        take(n, 0)
    for n in range(2, chips):
        ready(n, 0)
    early = dots(0, 0, 2)
    parts = [early]
    for n in range(1, chips - 1):
        take(n, 1)
        density(work[n + 1])
        weighed(n + 1)
        ready(n + 1, 1)
        parts.append(dots(0, n + 1, n + 2))
    gram = jnp.concatenate(parts, axis=1) + dots(1, 0, chips)
    index = lax.broadcasted_iota(jnp.int32, (total, total), 0)
    chip = jnp.zeros((total, total), jnp.int32)
    for n, p in enumerate(work):
        chip = jnp.where(index // both == n, p, chip)
    inside = lax.rem(index, per)
    far_core = lax.rem(index // per, 2)
    pick = (picks[...] == (2 * chip + c + far_core * (1 - 2 * c)) * per + inside).astype(jnp.float32)
    chosen = (picks[...] == (2 * chip + c) * per + inside).astype(jnp.float32)
    factor = 1.0 / jnp.sqrt(jnp.float32(planes * ns * ny * nz * norb))
    moved = lax.dot_general(
        pick, gram * factor, (((0,), (0,)), ((), ())), precision=lax.Precision.HIGH, preferred_element_type=jnp.float32
    )
    final = jnp.dot(moved, chosen, precision=lax.Precision.HIGH, preferred_element_type=jnp.float32)
    final = final + lax.dot_general(
        chosen, moved, (((0,), (1,)), ((), ())), precision=lax.Precision.HIGH, preferred_element_type=jnp.float32
    )
    owned = total // (nt * ns)
    for r in range(nt * ns):
        rows_out[r] = final[r * owned : (r + 1) * owned]
    if near:
        for j in range(1, nf):
            pl.semaphore_wait(gate, 1)

    def me():
        return (t * ns + s) * nf + f

    def row_copy(k):
        pt, ps, pf = device(k)
        return remote(
            rows_out.at[pt * ns + ps], rows_in.at[me()], row_s.at[0], row_r.at[0], trial=pt, slab=ps, freq=pf
        )

    def each(action):
        if count <= 64:
            for k in range(1, count):
                action(k)
        else:
            pl.loop(1, count)(action)

    each(lambda k: row_copy(k).start())
    rows_in[me()] = rows_out[t * ns + s]
    for j in range(1, nf):
        freq_copy(j).wait_send()
    when(up, lambda: pot_halo(0).wait_send())
    when(down, lambda: pot_halo(1).wait_send())
    for p in peers:

        def out_waits(rows):
            orb_out(p, rows).wait_send()
            shared(wide.at[p, :, inner, :rows, :], tri_s.at[p], tri_r.at[p, 0]).wait_send()

        sized(p, out_waits)
    shared(pars.at[: nt - 1], par_s.at[0], par_x.at[0]).wait_send()
    shared(other, fwd_s.at[0], fwd_r.at[0, 0]).wait_send()

    def sends(rows):
        n = short(rows)
        shared(orbs.at[some, inner, :rows, :], orb_s.at[chips], orb_x.at[0]).wait_send()

        @pl.when(up)
        def _():
            shared(orbs.at[some, under, :n, :], orb_s.at[chips + 1], orb_x.at[0]).wait_send()
            shared(orbs.at[some, over, :n, :], orb_s.at[chips + 4], orb_x.at[0]).wait_send()
            shared(wide.at[:, :, under, :n, :], fwd_s.at[1], orb_x.at[0]).wait_send()

        @pl.when(down)
        def _():
            shared(orbs.at[some, over, :n, :], orb_s.at[chips + 2], orb_x.at[0]).wait_send()
            shared(orbs.at[some, under, :n, :], orb_s.at[chips + 3], orb_x.at[0]).wait_send()
            shared(wide.at[:, :, over, :n, :], fwd_s.at[2], orb_x.at[0]).wait_send()

    sized(z, sends)
    rest = rows_in.at[: count - 1]
    remote(rest, rest, row_s.at[0], row_r.at[0], trial=mate).wait()
    out[...] = jnp.sum(rows_in[...], axis=0)


def local(sizes, orbitals, energies, potential, trials, cheb, shifts, column_order):
    nt, ns, nf = sizes
    per, planes, ny, nz = trials.shape
    norb = orbitals.shape[0] * nt
    chips = nt // 2
    mine = ny // nf // chips
    tall = -(-(mine + REACH) // 8) * 8
    deep = planes + UNDER + REACH
    total = nt * per
    owned = total // (nt * ns)
    count = nt * ns * nf
    f32 = jnp.float32
    dma = pltpu.SemaphoreType.DMA
    anywhere = pl.BlockSpec(memory_space=pltpu.HBM)
    return pl.pallas_call(
        functools.partial(kernel, sizes),
        out_shape=jax.ShapeDtypeStruct((owned, total), f32),
        in_specs=[anywhere] * 7,
        out_specs=pl.BlockSpec(memory_space=pltpu.VMEM),
        scratch_shapes=[
            pltpu.VMEM((norb, deep, tall, nz), f32),
            pltpu.VMEM((chips, per, deep, tall, nz), f32),
            pltpu.VMEM((chips, per, planes, mine, nz), f32),
            pltpu.VMEM((planes + 4, ny + 16, nz), f32),
            pltpu.VMEM((norb, 8, nz), f32),
            pltpu.VMEM((nf, 8, nz), f32),
            pltpu.VMEM((4, norb, 8, nz), f32),
            pltpu.VMEM((planes, len(OFFSETS), mine, nz), f32),
            pltpu.VMEM((chips, per, planes, mine, nz), f32),
            pltpu.VMEM((planes, total, mine * nz), jnp.bfloat16),
            pltpu.VMEM((planes, total, mine * nz), jnp.bfloat16),
            pltpu.VMEM((planes, total, mine * nz), jnp.bfloat16),
            pltpu.VMEM((nt * ns, owned, total), f32),
            pltpu.VMEM((count, owned, total), f32),
            pltpu.SMEM((1,), f32),
            pltpu.SMEM((1, 4), f32),
            pltpu.SMEM((1,), f32),
            pltpu.VMEM((1, total), jnp.int32),
            dma((chips + 5,)), dma((chips, 3)), dma((3,)), dma((1,)), dma((chips,)), dma((1,)),
            dma((2,)), dma((2,)), dma((nf,)), dma((nf,)),
            dma((chips,)), dma((chips, PIECES)), dma((3,)), dma((chips, 4)),
            dma((1,)), dma((1,)),
            dma((7,)),
            pltpu.SemaphoreType.REGULAR,
        ],
        compiler_params=pltpu.CompilerParams(
            collective_id=0, has_side_effects=True, vmem_limit_bytes=67043328 - 65536
        ),
    )(orbitals, energies, potential, trials, cheb, shifts, column_order[None])


def solution(mesh):
    sizes = tuple(mesh.shape[name] for name in ("trial", "slab", "freq"))
    in_specs = (
        P("trial", "slab", None, None),
        P("trial"),
        P("slab", None, None),
        P("trial", "slab", None, None),
        P("freq", None),
        P("freq"),
        P(),
    )
    out_specs = P(("trial", "slab"), None)
    return jax.shard_map(
        functools.partial(local, sizes), mesh=mesh, in_specs=in_specs, out_specs=out_specs, check_vma=False
    )
```
